32 devices in a mesh: gx: 8 (over z, x), gy: 4 (over y, core).
Axes of the slice: x: 2, y: 2, z: 4, core: 2. Of those that a mesh axis runs over, the one named last changes fastest.
Arguments:
- tangent: float32 [128, 64, 512], P('gx', 'gy'), may hold values from -6 to 6
- hessian: bfloat16 [5, 5, 128, 64, 512], P(None, None, 'gx', 'gy'), may hold values from -1.5 to 8, as said below
- kernel_rows: float32 [5, 17], replicated, may hold values from -1 to 1
- kernel_cols: float32 [5, 17], replicated, may hold values from -1 to 1
- kernel_depth: bfloat16 [5, 17], replicated, may hold values from -1 to 1
Outputs:
- hessian_product: float32 [128, 64, 512], P('gx', 'gy')
The draws below stay inside these ranges and needn't reach their ends.
Inputs may be any that keep to these rules, and one draw needn't show every extreme that they name: `hessian`: Off-diagonal entries lie within -1.5 to 1.5; diagonal entries are positive, between 0.3 and 8.
All inputs are finite; a program needn't handle non-finite values.
Results may differ from the reference program's by a relative error of at most 0.0022.
Values sent between devices are 32-bit elements; how exact they have to be, the bound alone decides.
A program may use at most 128 MiB of HBM per device.

```python
import jax
import jax.numpy as jnp
from jax import lax

NZ = 512
RADIUS = 8
DENSITIES = 5
TAPS = 17
NX = 128
NY = 64


def draw_hessian(key, part):
    first_key, second_key = jax.random.split(jax.random.fold_in(key, 17))
    full_shape = (DENSITIES, DENSITIES, NX, NY, NZ)
    diag_shape = (DENSITIES, 1, NX, NY, NZ)
    offdiag = jnp.clip(0.3 * jax.random.normal(first_key, full_shape, jnp.float32), -1.5, 1.5)
    diagonal = jnp.exp(jax.random.uniform(second_key, diag_shape, jnp.float32, jnp.log(0.5), jnp.log(5.0)))
    identity = jnp.eye(DENSITIES, dtype=jnp.float32)[:, :, None, None, None]
    return (offdiag * (1.0 - identity) + diagonal * identity).astype(jnp.bfloat16)


def levels(own_key, dims, cuts, least, high):
    def one(dim, parts):
        steps = jax.random.uniform(jax.random.fold_in(jax.random.fold_in(own_key, 6), dim), (parts,), jnp.float32, least / len(cuts), high / len(cuts))
        return jnp.repeat(jnp.exp(steps), dims[dim] // parts).reshape((-1,) + (1,) * (len(dims) - dim - 1))

    level = one(*cuts[0])
    for cut in cuts[1:]:
        level = level * one(*cut)
    return level


def noise(stream_key, shape, width, limit, shards=(), kind=jnp.bfloat16):
    drawn = width * jax.random.normal(stream_key, shape, jnp.float32)
    if shards:
        drawn = drawn * levels(stream_key, shape, shards, -0.22, 0.18)
    return jnp.clip(drawn, -limit, limit).astype(kind)


def setup_inputs(seed: int = 0) -> dict:
    seeds = jax.random.split(jax.random.key(seed), 6)
    return {
        "tangent": noise(seeds[0], (NX, NY, NZ), 1.0, 6.0, ((0, 8), (1, 4)), jnp.float32),
        "hessian": draw_hessian(jax.random.fold_in(seeds[5], 71), 0),
        "kernel_rows": noise(seeds[2], (DENSITIES, TAPS), 0.24, 1.0, (), jnp.float32),
        "kernel_cols": noise(seeds[3], (DENSITIES, TAPS), 0.24, 1.0, (), jnp.float32),
        "kernel_depth": noise(seeds[4], (DENSITIES, TAPS), 0.24, 1.0),
    }


def lateral_forward(field, weights, axis_number):
    total = jnp.zeros_like(field)
    for shift_tap in range(2 * RADIUS + 1):
        total = total + weights[shift_tap] * jnp.roll(field, RADIUS - shift_tap, axis_number)
    return total


def lateral_transpose(field, weights, axis_number):
    total = jnp.zeros_like(field)
    for shift_tap in range(2 * RADIUS + 1):
        total = total + weights[shift_tap] * jnp.roll(field, shift_tap - RADIUS, axis_number)
    return total


def widen(field):
    rounded = lax.optimization_barrier(field.astype(jnp.bfloat16))
    return rounded.astype(jnp.float32)


def depth_forward(field, weights):
    padded = jnp.pad(field, ((0, 0), (0, 0), (RADIUS, RADIUS)))
    total = jnp.zeros(field.shape, jnp.float32)
    for shift_tap in range(2 * RADIUS + 1):
        total = total + weights[shift_tap].astype(jnp.float32) * padded[:, :, shift_tap:shift_tap + NZ]
    return total


def depth_transpose(field, weights):
    padded = jnp.pad(field, ((0, 0), (0, 0), (RADIUS, RADIUS)))
    total = jnp.zeros(field.shape, jnp.float32)
    for shift_tap in range(2 * RADIUS + 1):
        start = 2 * RADIUS - shift_tap
        total = total + weights[shift_tap].astype(jnp.float32) * padded[:, :, start:start + NZ]
    return total


def reference(tangent, hessian, kernel_rows, kernel_cols, kernel_depth):
    densities = []
    for density in range(DENSITIES):
        field = lateral_forward(tangent, kernel_rows[density], 0)
        field = lateral_forward(field, kernel_cols[density], 1)
        densities.append(depth_forward(widen(field), kernel_depth[density]))
    result = jnp.zeros_like(tangent)
    for density in range(DENSITIES):
        gradient = jnp.zeros_like(tangent)
        for other in range(DENSITIES):
            gradient = gradient + hessian[density, other].astype(jnp.float32) * densities[other]
        field = depth_transpose(widen(gradient), kernel_depth[density])
        field = lateral_transpose(field, kernel_rows[density], 0)
        field = lateral_transpose(field, kernel_cols[density], 1)
        result = result + field
    return result
```

```python
import jax
import jax.numpy as jnp
from jax import lax
from jax.experimental import pallas as pl
from jax.experimental.pallas import tpu as pltpu
from jax.sharding import PartitionSpec as P

RADIUS = 8
DENSITIES = 5
TAPS = 2 * RADIUS + 1
LANES = 128
WINDOW = 2 * LANES


def split(value):
    high = value.astype(jnp.bfloat16)
    low = (value - high.astype(jnp.float32)).astype(jnp.bfloat16)
    return high, low


def dot(left, right):
    return jnp.dot(left, right, preferred_element_type=jnp.float32)


def dot3(left_high, left_low, right_high, right_low):
    return dot(left_high, right_high) + dot(left_high, right_low) + dot(left_low, right_high)


def picked(taps, index):
    total = jnp.zeros(index.shape, jnp.float32)
    for tap in range(TAPS):
        weight = jnp.broadcast_to(taps[:, tap : tap + 1], index.shape)
        total = jnp.where(index == tap, weight, total)
    return total


def iota(shape, axis):
    return lax.broadcasted_iota(jnp.int32, shape, axis)


def build_forward(sizes, rows, cols, high_ref, low_ref):
    span_cols, ext_cols = sizes[1], sizes[3]
    wide = 3 * RADIUS * ext_cols
    row_index = iota((RADIUS, wide), 1) // ext_cols - iota((RADIUS, wide), 0)
    col_index = iota((span_cols, LANES), 1) % ext_cols - iota((span_cols, LANES), 0)
    for a in range(DENSITIES):
        by_row = picked(rows[a : a + 1], row_index)
        by_col = picked(cols[a : a + 1], col_index)
        by_col = jnp.concatenate([by_col] * (wide // LANES), axis=1)
        for r in range(RADIUS):
            at = pl.ds((a * RADIUS + r) * span_cols, span_cols)
            high_ref[at, :], low_ref[at, :] = split(by_row[r : r + 1, :] * by_col)


def build_backward(sizes, rows, cols, high_ref, low_ref):
    span_cols, ext_cols = sizes[1], sizes[3]
    size = RADIUS * span_cols
    row_index = iota((3 * RADIUS, size), 0) - iota((3 * RADIUS, size), 1) // span_cols
    col_index = iota((ext_cols, size), 0) - iota((ext_cols, size), 1) % span_cols
    for a in range(DENSITIES):
        by_row = picked(rows[a : a + 1], row_index)
        by_col = picked(cols[a : a + 1], col_index)
        into = pl.ds(a * size, size)
        for r in range(3 * RADIUS):
            at = pl.ds(r * ext_cols, ext_cols)
            high_ref[at, into], low_ref[at, into] = split(by_row[r : r + 1, :] * by_col)


def build_bands(depth_taps, band_ref, band_t_ref):
    step = 16
    shape = (step, WINDOW)
    offset = iota(shape, 0) - iota(shape, 1)
    for a in range(DENSITIES):
        taps = depth_taps[a : a + 1]
        for ref, sign in ((band_ref, 1), (band_t_ref, -1)):
            middle = picked(taps, sign * (offset + LANES) + RADIUS)
            for i in range(WINDOW // step):
                value = pltpu.roll(middle, (step * i - LANES) % WINDOW, 1)
                if i in (0, WINDOW // step - 1):
                    value = jnp.where(jnp.abs(offset + step * i) <= RADIUS, value, 0.0)
                ref[a, pl.ds(i * step, step), :] = value.astype(jnp.bfloat16)


def compute(sizes, counts, tangent_ref, hess_ref, rows_ref, cols_ref, depth_ref, out_ref,
            ext, high, low, fwd_high, fwd_low, bwd_high, bwd_low, band, band_t, hess,
            acc, lateral, dens, lowered, pending, back_high, back_low, spread,
            from_left, from_right, from_up, from_down,
            local_sems, out_sems, send_sems, recv_sems, back_send_sems, back_recv_sems):
    span_rows, span_cols, ext_rows, ext_cols = sizes
    depth = acc.shape[-1]
    reach = RADIUS
    groups = span_rows // reach
    own, size, block = span_rows * span_cols, reach * span_cols, reach * ext_cols
    chunks = depth // LANES
    gx, gy = lax.axis_index("gx"), lax.axis_index("gy")
    up = {"gx": lax.rem(gx + counts[0] - 1, counts[0])}
    down = {"gx": lax.rem(gx + 1, counts[0])}
    left = {"gy": lax.rem(gy + counts[1] - 1, counts[1])}
    right = {"gy": lax.rem(gy + 1, counts[1])}
    mesh_ids = pl.DeviceIdType.MESH

    inner_rows, inner_cols = pl.ds(reach, span_rows), pl.ds(reach, span_cols)
    barrier = pltpu.get_barrier_semaphore()
    for neighbour in (up, down, left, right):
        pl.semaphore_signal(barrier, inc=1, device_id=neighbour, device_id_type=mesh_ids)
    fetch = pltpu.make_async_copy(hess_ref, hess, local_sems.at[0])
    home = pltpu.make_async_copy(tangent_ref, ext.at[inner_rows, inner_cols, :], local_sems.at[1])
    home.start()
    pl.semaphore_wait(barrier, 4)

    first, last = pl.ds(0, reach), pl.ds(reach + span_rows, reach)
    first_cols, last_cols = pl.ds(0, reach), pl.ds(reach + span_cols, reach)
    near_first, near_last = pl.ds(reach, reach), pl.ds(span_cols, reach)
    lanes = [pl.ds(c * LANES, LANES) for c in range(chunks)]

    def remote(source, target, send_sem, recv_sem, device):
        return pltpu.make_async_remote_copy(
            src_ref=source, dst_ref=target, send_sem=send_sem, recv_sem=recv_sem,
            device_id=device, device_id_type=mesh_ids)

    head_rows, tail_rows = pl.ds(0, reach), pl.ds(span_rows - reach, reach)
    head_cols, tail_cols = pl.ds(0, reach), pl.ds(span_cols - reach, reach)
    every_row, every_col = pl.ds(0, span_rows), pl.ds(0, span_cols)
    copies, returns = {}, {}
    for c, z in enumerate(lanes):
        plan = [
            (tangent_ref.at[tail_rows, every_col, z], ext.at[first, inner_cols, z], down),
            (tangent_ref.at[head_rows, every_col, z], ext.at[last, inner_cols, z], up),
            (tangent_ref.at[every_row, tail_cols, z], ext.at[inner_rows, first_cols, z], right),
            (tangent_ref.at[every_row, head_cols, z], ext.at[inner_rows, last_cols, z], left),
        ]
        for rows_at in (first, last):
            plan.append((ext.at[rows_at, near_last, z], ext.at[rows_at, first_cols, z], right))
            plan.append((ext.at[rows_at, near_first, z], ext.at[rows_at, last_cols, z], left))
        for kind, (source, target, device) in enumerate(plan):
            copies[kind, c] = remote(source, target, send_sems.at[kind, c], recv_sems.at[kind, c], device)
        plan = []
        for rows_at in (first, last, inner_rows):
            plan.append((spread.at[rows_at, last_cols, z], from_left.at[rows_at, :, z], right))
            plan.append((spread.at[rows_at, first_cols, z], from_right.at[rows_at, :, z], left))
        plan.append((spread.at[first, inner_cols, z], from_down.at[:, :, z], up))
        plan.append((spread.at[last, inner_cols, z], from_up.at[:, :, z], down))
        for kind, (source, target, device) in enumerate(plan):
            returns[kind, c] = remote(source, target, back_send_sems.at[kind, c], back_recv_sems.at[kind, c], device)
    for c in range(chunks):
        for kind in range(4):
            copies[kind, c].start()
    fetch.start()

    def relay(c):
        for kind in (0, 1):
            copies[kind, c].wait_recv()
        for kind in (4, 5, 6, 7):
            copies[kind, c].start()

    def prepare(z, begin, count):
        value = ext[pl.ds(begin * reach, count * reach), :, z].reshape(count * block, z.size)
        at = pl.ds(begin * block, count * block)
        high[at, z], low[at, z] = split(value)

    def product(group, begin, end, z):
        weights, data = pl.ds((begin - group) * block, (end - begin) * block), pl.ds(begin * block, (end - begin) * block)
        return dot3(fwd_high[:, weights], fwd_low[:, weights], high[data, z], low[data, z])

    def middle(begin, end):
        z = pl.ds(begin * LANES, (end - begin) * LANES)
        for c in range(begin, end):
            copies[2, c].wait_recv()
            copies[3, c].wait_recv()
        prepare(z, 1, groups)
        for group in range(groups):
            acc[group, :, z] = product(group, max(group, 1), min(group + 3, groups + 1), z)

    def edges(begin, end):
        z = pl.ds(begin * LANES, (end - begin) * LANES)
        for c in range(begin, end):
            for kind in (4, 5, 6, 7):
                copies[kind, c].wait_recv()
        prepare(z, 0, 1)
        prepare(z, groups + 1, 1)
        for group in range(groups):
            total = acc[group, :, z]
            if group == 0:
                total = total + product(group, 0, 1, z)
            if group == groups - 1:
                total = total + product(group, groups + 1, groups + 2, z)
            total = total.astype(jnp.bfloat16)
            for a in range(DENSITIES):
                lateral[a, pl.ds(group * size, size), z] = total[a * size : (a + 1) * size]

    keep = iota((own, LANES), 1) < LANES // 2

    def along_depth(k):
        z, here, ahead = pl.ds(k * LANES, WINDOW), lanes[k], lanes[k + 1]
        for a in range(DENSITIES):
            value = dot(lateral[a, :, z], band[a])
            begin = value[:, :LANES]
            dens[a, :, here] = begin if k == 0 else jnp.where(keep, dens[a, :, here], begin)
            dens[a, :, ahead] = value[:, LANES:]

    def gradient(k):
        step = 16

        def piece(i, carry):
            at = pl.ds(pl.multiple_of(i * step, step), step)
            for z in (lanes[k], lanes[k + 1]):
                values = [dens[b, at, z] for b in range(DENSITIES)]
                for a in range(DENSITIES):
                    total = None
                    for b in range(DENSITIES):
                        term = hess[a, b, at, z].astype(jnp.float32) * values[b]
                        total = term if total is None else total + term
                    lowered[a, at, z] = total.astype(jnp.bfloat16)
            return carry

        lax.fori_loop(0, own // step, piece, 0)

    def against_depth(k):
        z, here, ahead = pl.ds(k * LANES, WINDOW), lanes[k], lanes[k + 1]

        def finish(a, value, target):
            value_high, value_low = split(value)
            for group in range(groups):
                part = pl.ds(a * size, size)
                back_high[group, part, target] = value_high[group * size : (group + 1) * size]
                back_low[group, part, target] = value_low[group * size : (group + 1) * size]

        for a in range(DENSITIES):
            value = dot(lowered[a, :, z], band_t[a])
            begin = value[:, :LANES]
            finish(a, begin if k == 0 else jnp.where(keep, pending[a], begin), here)
            if k == chunks - 2:
                finish(a, value[:, LANES:], ahead)
            else:
                pending[a] = value[:, LANES:]

    def spread_block(index, z):
        total = None
        for group in range(groups):
            if 0 <= index - group < 3:
                part = pl.ds((index - group) * block, block)
                term = dot3(bwd_high[part, :], bwd_low[part, :], back_high[group, :, z], back_low[group, :, z])
                total = term if total is None else total + term
        spread[pl.ds(index * reach, reach), :, z] = total.reshape(reach, ext_cols, z.size)

    def corners(begin, end):
        z = pl.ds(begin * LANES, (end - begin) * LANES)
        spread_block(0, z)
        spread_block(groups + 1, z)
        for c in range(begin, end):
            for kind in (0, 1, 2, 3):
                returns[kind, c].start()

    def sides(begin, end):
        z = pl.ds(begin * LANES, (end - begin) * LANES)
        for index in range(1, groups + 1):
            spread_block(index, z)
        for c in range(begin, end):
            for kind in (4, 5):
                returns[kind, c].start()

    def strips(c):
        z = lanes[c]
        for kind, rows_at, strip in ((0, first, 6), (2, last, 7)):
            returns[kind, c].wait_recv()
            returns[kind + 1, c].wait_recv()
            spread[rows_at, near_first, z] = spread[rows_at, near_first, z] + from_left[rows_at, :, z]
            spread[rows_at, near_last, z] = spread[rows_at, near_last, z] + from_right[rows_at, :, z]
            returns[strip, c].start()

    def final(c):
        z = lanes[c]
        for kind in (4, 5, 6, 7):
            returns[kind, c].wait_recv()
        spread[inner_rows, near_first, z] = spread[inner_rows, near_first, z] + from_left[inner_rows, :, z]
        spread[inner_rows, near_last, z] = spread[inner_rows, near_last, z] + from_right[inner_rows, :, z]
        top, bottom = pl.ds(reach, reach), pl.ds(span_rows, reach)
        spread[top, inner_cols, z] = spread[top, inner_cols, z] + from_up[:, :, z]
        spread[bottom, inner_cols, z] = spread[bottom, inner_cols, z] + from_down[:, :, z]
        copy = pltpu.make_async_copy(spread.at[inner_rows, inner_cols, z], out_ref.at[:, :, z], out_sems.at[c])
        copy.start()
        return copy

    rows, cols = rows_ref[...], cols_ref[...]
    build_forward(sizes, rows, cols, fwd_high, fwd_low)
    build_bands(depth_ref[...].astype(jnp.float32), band, band_t)
    build_backward(sizes, rows, cols, bwd_high, bwd_low)
    home.wait()
    relay(0)
    middle(0, 2)
    relay(1)
    for c in range(2, chunks, 2):
        middle(c, min(c + 2, chunks))
    edges(0, 2)
    relayed = 2
    fetch.wait()
    for k in range(chunks - 1):
        if k > 0:
            edges(k + 1, k + 2)
        if relayed < chunks:
            relay(relayed)
            relayed += 1
        along_depth(k)
        gradient(k)
        if k > 0:
            strips(k - 1)
        against_depth(k)
        final_step = k == chunks - 2
        corners(k, chunks if final_step else k + 1)
        if relayed < chunks:
            relay(relayed)
            relayed += 1
        sides(k, chunks if final_step else k + 1)
    strips(chunks - 2)
    strips(chunks - 1)
    outs = [final(c) for c in range(chunks)]
    for copy in list(copies.values()) + list(returns.values()):
        copy.wait_send()
    for copy in outs:
        copy.wait()


def per_device(tangent, hessian, kernel_rows, kernel_cols, kernel_depth):
    span_rows, span_cols, depth = tangent.shape
    reach = RADIUS
    ext_rows, ext_cols = span_rows + 2 * reach, span_cols + 2 * reach
    sizes = (span_rows, span_cols, ext_rows, ext_cols)
    counts = (lax.axis_size("gx"), lax.axis_size("gy"))
    own, wide = span_rows * span_cols, ext_rows * ext_cols
    groups, size, block = span_rows // reach, reach * span_cols, reach * ext_cols
    chunks = depth // LANES
    full = pl.BlockSpec(memory_space=pltpu.VMEM)
    anywhere = pl.BlockSpec(memory_space=pl.ANY)
    bf16, f32 = jnp.bfloat16, jnp.float32
    return pl.pallas_call(
        lambda *refs: compute(sizes, counts, *refs),
        out_shape=jax.ShapeDtypeStruct((span_rows, span_cols, depth), f32),
        in_specs=[anywhere, anywhere, full, full, full],
        out_specs=anywhere,
        scratch_shapes=[
            pltpu.VMEM((ext_rows, ext_cols, depth), f32),
            pltpu.VMEM((wide, depth), bf16),
            pltpu.VMEM((wide, depth), bf16),
            pltpu.VMEM((DENSITIES * size, 3 * block), bf16),
            pltpu.VMEM((DENSITIES * size, 3 * block), bf16),
            pltpu.VMEM((3 * block, DENSITIES * size), bf16),
            pltpu.VMEM((3 * block, DENSITIES * size), bf16),
            pltpu.VMEM((DENSITIES, WINDOW, WINDOW), bf16),
            pltpu.VMEM((DENSITIES, WINDOW, WINDOW), bf16),
            pltpu.VMEM((DENSITIES, DENSITIES, own, depth), bf16),
            pltpu.VMEM((groups, DENSITIES * size, depth), f32),
            pltpu.VMEM((DENSITIES, own, depth), bf16),
            pltpu.VMEM((DENSITIES, own, depth), f32),
            pltpu.VMEM((DENSITIES, own, depth), bf16),
            pltpu.VMEM((DENSITIES, own, LANES), f32),
            pltpu.VMEM((groups, DENSITIES * size, depth), bf16),
            pltpu.VMEM((groups, DENSITIES * size, depth), bf16),
            pltpu.VMEM((ext_rows, ext_cols, depth), f32),
            pltpu.VMEM((ext_rows, reach, depth), f32),
            pltpu.VMEM((ext_rows, reach, depth), f32),
            pltpu.VMEM((reach, span_cols, depth), f32),
            pltpu.VMEM((reach, span_cols, depth), f32),
            pltpu.SemaphoreType.DMA((2,)),
            pltpu.SemaphoreType.DMA((chunks,)),
            pltpu.SemaphoreType.DMA((8, chunks)),
            pltpu.SemaphoreType.DMA((8, chunks)),
            pltpu.SemaphoreType.DMA((8, chunks)),
            pltpu.SemaphoreType.DMA((8, chunks)),
        ],
        compiler_params=pltpu.CompilerParams(
            vmem_limit_bytes=60 << 20, collective_id=0, has_side_effects=True),
    )(tangent, hessian.reshape(DENSITIES, DENSITIES, own, depth), kernel_rows, kernel_cols, kernel_depth)


def solution(mesh):
    return jax.shard_map(
        per_device,
        mesh=mesh,
        in_specs=(P("gx", "gy", None), P(None, None, "gx", "gy", None), P(), P(), P()),
        out_specs=P("gx", "gy", None),
        check_vma=False,
    )
```

```python
import jax
import jax.numpy as jnp
from jax import lax
from jax.experimental import pallas as pl
from jax.experimental.pallas import tpu as pltpu
from jax.sharding import PartitionSpec as P

RADIUS = 8
DENSITIES = 5
TAPS = 2 * RADIUS + 1
LANES = 128
WINDOW = 2 * LANES


def split(value):
    high = value.astype(jnp.bfloat16)
    low = (value - high.astype(jnp.float32)).astype(jnp.bfloat16)
    return high, low


def dot(left, right):
    return jnp.dot(left, right, preferred_element_type=jnp.float32)


def dot3(left_high, left_low, right_high, right_low):
    return dot(left_high, right_high) + dot(left_high, right_low) + dot(left_low, right_high)


def picked(taps, index):
    total = jnp.zeros(index.shape, jnp.float32)
    for tap in range(TAPS):
        weight = jnp.broadcast_to(taps[:, tap : tap + 1], index.shape)
        total = jnp.where(index == tap, weight, total)
    return total


def iota(shape, axis):
    return lax.broadcasted_iota(jnp.int32, shape, axis)


def build_forward(sizes, rows, cols, high_ref, low_ref):
    span_cols, ext_cols = sizes[1], sizes[3]
    wide = 3 * RADIUS * ext_cols
    row_index = iota((RADIUS, wide), 1) // ext_cols - iota((RADIUS, wide), 0)
    col_index = iota((span_cols, LANES), 1) % ext_cols - iota((span_cols, LANES), 0)
    for a in range(DENSITIES):
        by_row = picked(rows[a : a + 1], row_index)
        by_col = picked(cols[a : a + 1], col_index)
        by_col = jnp.concatenate([by_col] * (wide // LANES), axis=1)
        for r in range(RADIUS):
            at = pl.ds((a * RADIUS + r) * span_cols, span_cols)
            high_ref[at, :], low_ref[at, :] = split(by_row[r : r + 1, :] * by_col)


def build_backward(sizes, rows, cols, high_ref, low_ref):
    span_cols, ext_cols = sizes[1], sizes[3]
    size = RADIUS * span_cols
    row_index = iota((3 * RADIUS, size), 0) - iota((3 * RADIUS, size), 1) // span_cols
    col_index = iota((ext_cols, size), 0) - iota((ext_cols, size), 1) % span_cols
    for a in range(DENSITIES):
        by_row = picked(rows[a : a + 1], row_index)
        by_col = picked(cols[a : a + 1], col_index)
        into = pl.ds(a * size, size)
        for r in range(3 * RADIUS):
            at = pl.ds(r * ext_cols, ext_cols)
            high_ref[at, into], low_ref[at, into] = split(by_row[r : r + 1, :] * by_col)


def build_bands(depth_taps, band_ref, band_t_ref):
    step = 16
    shape = (step, WINDOW)
    offset = iota(shape, 0) - iota(shape, 1)
    for a in range(DENSITIES):
        taps = depth_taps[a : a + 1]
        for ref, sign in ((band_ref, 1), (band_t_ref, -1)):
            middle = picked(taps, sign * (offset + LANES) + RADIUS)
            for i in range(WINDOW // step):
                value = pltpu.roll(middle, (step * i - LANES) % WINDOW, 1)
                if i in (0, WINDOW // step - 1):
                    value = jnp.where(jnp.abs(offset + step * i) <= RADIUS, value, 0.0)
                ref[a, pl.ds(i * step, step), :] = value.astype(jnp.bfloat16)


def compute(sizes, counts, tangent_ref, hess_ref, rows_ref, cols_ref, depth_ref, out_ref,
            ext, high, low, fwd_high, fwd_low, bwd_high, bwd_low, band, band_t, hess,
            acc, lateral, dens, lowered, pending, back_high, back_low, spread,
            from_left, from_right, from_up, from_down,
            local_sems, out_sems, send_sems, recv_sems, back_send_sems, back_recv_sems):
    span_rows, span_cols, ext_rows, ext_cols = sizes
    depth = acc.shape[-1]
    reach = RADIUS
    groups = span_rows // reach
    own, size, block = span_rows * span_cols, reach * span_cols, reach * ext_cols
    chunks = depth // LANES
    gx, gy = lax.axis_index("gx"), lax.axis_index("gy")
    up = {"gx": lax.rem(gx + counts[0] - 1, counts[0])}
    down = {"gx": lax.rem(gx + 1, counts[0])}
    left = {"gy": lax.rem(gy + counts[1] - 1, counts[1])}
    right = {"gy": lax.rem(gy + 1, counts[1])}
    mesh_ids = pl.DeviceIdType.MESH

    inner_rows, inner_cols = pl.ds(reach, span_rows), pl.ds(reach, span_cols)
    barrier = pltpu.get_barrier_semaphore()
    for neighbour in (up, down, left, right):
        pl.semaphore_signal(barrier, inc=1, device_id=neighbour, device_id_type=mesh_ids)
    fetch = pltpu.make_async_copy(hess_ref, hess, local_sems.at[0])
    home = pltpu.make_async_copy(tangent_ref, ext.at[inner_rows, inner_cols, :], local_sems.at[1])
    home.start()
    pl.semaphore_wait(barrier, 4)

    first, last = pl.ds(0, reach), pl.ds(reach + span_rows, reach)
    first_cols, last_cols = pl.ds(0, reach), pl.ds(reach + span_cols, reach)
    near_first, near_last = pl.ds(reach, reach), pl.ds(span_cols, reach)
    lanes = [pl.ds(c * LANES, LANES) for c in range(chunks)]

    def remote(source, target, send_sem, recv_sem, device):
        return pltpu.make_async_remote_copy(
            src_ref=source, dst_ref=target, send_sem=send_sem, recv_sem=recv_sem,
            device_id=device, device_id_type=mesh_ids)

    head_rows, tail_rows = pl.ds(0, reach), pl.ds(span_rows - reach, reach)
    head_cols, tail_cols = pl.ds(0, reach), pl.ds(span_cols - reach, reach)
    every_row, every_col = pl.ds(0, span_rows), pl.ds(0, span_cols)
    copies, returns = {}, {}
    for c, z in enumerate(lanes):
        plan = [
            (tangent_ref.at[tail_rows, every_col, z], ext.at[first, inner_cols, z], down),
            (tangent_ref.at[head_rows, every_col, z], ext.at[last, inner_cols, z], up),
            (tangent_ref.at[every_row, tail_cols, z], ext.at[inner_rows, first_cols, z], right),
            (tangent_ref.at[every_row, head_cols, z], ext.at[inner_rows, last_cols, z], left),
        ]
        for rows_at in (first, last):
            plan.append((ext.at[rows_at, near_last, z], ext.at[rows_at, first_cols, z], right))
            plan.append((ext.at[rows_at, near_first, z], ext.at[rows_at, last_cols, z], left))
        for kind, (source, target, device) in enumerate(plan):
            copies[kind, c] = remote(source, target, send_sems.at[kind, c], recv_sems.at[kind, c], device)
        plan = []
        for rows_at in (first, last, inner_rows):
            plan.append((spread.at[rows_at, last_cols, z], from_left.at[rows_at, :, z], right))
            plan.append((spread.at[rows_at, first_cols, z], from_right.at[rows_at, :, z], left))
        plan.append((spread.at[first, inner_cols, z], from_down.at[:, :, z], up))
        plan.append((spread.at[last, inner_cols, z], from_up.at[:, :, z], down))
        for kind, (source, target, device) in enumerate(plan):
            returns[kind, c] = remote(source, target, back_send_sems.at[kind, c], back_recv_sems.at[kind, c], device)
    def relay(c):
        for kind in (0, 1):
            copies[kind, c].wait_recv()
        for kind in (4, 5, 6, 7):
            copies[kind, c].start()

    def prepare(z, begin, count):
        value = ext[pl.ds(begin * reach, count * reach), :, z].reshape(count * block, z.size)
        at = pl.ds(begin * block, count * block)
        high[at, z], low[at, z] = split(value)

    def product(group, begin, end, z):
        weights, data = pl.ds((begin - group) * block, (end - begin) * block), pl.ds(begin * block, (end - begin) * block)
        return dot3(fwd_high[:, weights], fwd_low[:, weights], high[data, z], low[data, z])

    def middle(begin, end):
        z = pl.ds(begin * LANES, (end - begin) * LANES)
        for c in range(begin, end):
            copies[2, c].wait_recv()
            copies[3, c].wait_recv()
        prepare(z, 1, groups)
        for group in range(groups):
            acc[group, :, z] = product(group, max(group, 1), min(group + 3, groups + 1), z)

    def edges(begin, end):
        z = pl.ds(begin * LANES, (end - begin) * LANES)
        for c in range(begin, end):
            for kind in (4, 5, 6, 7):
                copies[kind, c].wait_recv()
        prepare(z, 0, 1)
        prepare(z, groups + 1, 1)
        for group in range(groups):
            total = acc[group, :, z]
            if group == 0:
                total = total + product(group, 0, 1, z)
            if group == groups - 1:
                total = total + product(group, groups + 1, groups + 2, z)
            total = total.astype(jnp.bfloat16)
            for a in range(DENSITIES):
                lateral[a, pl.ds(group * size, size), z] = total[a * size : (a + 1) * size]

    keep = iota((own, LANES), 1) < LANES // 2

    def along_depth(k):
        z, here, ahead = pl.ds(k * LANES, WINDOW), lanes[k], lanes[k + 1]
        for a in range(DENSITIES):
            value = dot(lateral[a, :, z], band[a])
            begin = value[:, :LANES]
            dens[a, :, here] = begin if k == 0 else jnp.where(keep, dens[a, :, here], begin)
            dens[a, :, ahead] = value[:, LANES:]

    def gradient(k):
        step = 16

        def piece(i, carry):
            at = pl.ds(pl.multiple_of(i * step, step), step)
            for z in (lanes[k], lanes[k + 1]):
                values = [dens[b, at, z] for b in range(DENSITIES)]
                for a in range(DENSITIES):
                    total = None
                    for b in range(DENSITIES):
                        term = hess[a, b, at, z].astype(jnp.float32) * values[b]
                        total = term if total is None else total + term
                    lowered[a, at, z] = total.astype(jnp.bfloat16)
            return carry

        lax.fori_loop(0, own // step, piece, 0, unroll=4)

    def against_depth(k):
        z, here, ahead = pl.ds(k * LANES, WINDOW), lanes[k], lanes[k + 1]

        def finish(a, value, target):
            value_high, value_low = split(value)
            for group in range(groups):
                part = pl.ds(a * size, size)
                back_high[group, part, target] = value_high[group * size : (group + 1) * size]
                back_low[group, part, target] = value_low[group * size : (group + 1) * size]

        for a in range(DENSITIES):
            value = dot(lowered[a, :, z], band_t[a])
            begin = value[:, :LANES]
            finish(a, begin if k == 0 else jnp.where(keep, pending[a], begin), here)
            if k == chunks - 2:
                finish(a, value[:, LANES:], ahead)
            else:
                pending[a] = value[:, LANES:]

    def spread_block(index, z):
        total = None
        for group in range(groups):
            if 0 <= index - group < 3:
                part = pl.ds((index - group) * block, block)
                term = dot3(bwd_high[part, :], bwd_low[part, :], back_high[group, :, z], back_low[group, :, z])
                total = term if total is None else total + term
        spread[pl.ds(index * reach, reach), :, z] = total.reshape(reach, ext_cols, z.size)

    def corners(begin, end):
        z = pl.ds(begin * LANES, (end - begin) * LANES)
        spread_block(0, z)
        spread_block(groups + 1, z)
        for c in range(begin, end):
            for kind in (0, 1, 2, 3):
                returns[kind, c].start()

    def sides(begin, end):
        z = pl.ds(begin * LANES, (end - begin) * LANES)
        for index in range(1, groups + 1):
            spread_block(index, z)
        for c in range(begin, end):
            for kind in (4, 5):
                returns[kind, c].start()

    def strips(c):
        z = lanes[c]
        for kind, rows_at, strip in ((0, first, 6), (2, last, 7)):
            returns[kind, c].wait_recv()
            returns[kind + 1, c].wait_recv()
            spread[rows_at, near_first, z] = spread[rows_at, near_first, z] + from_left[rows_at, :, z]
            spread[rows_at, near_last, z] = spread[rows_at, near_last, z] + from_right[rows_at, :, z]
            returns[strip, c].start()

    def final(c):
        z = lanes[c]
        for kind in (4, 5, 6, 7):
            returns[kind, c].wait_recv()
        spread[inner_rows, near_first, z] = spread[inner_rows, near_first, z] + from_left[inner_rows, :, z]
        spread[inner_rows, near_last, z] = spread[inner_rows, near_last, z] + from_right[inner_rows, :, z]
        top, bottom = pl.ds(reach, reach), pl.ds(span_rows, reach)
        spread[top, inner_cols, z] = spread[top, inner_cols, z] + from_up[:, :, z]
        spread[bottom, inner_cols, z] = spread[bottom, inner_cols, z] + from_down[:, :, z]
        out_ref[:, :, z] = spread[inner_rows, inner_cols, z]

    copies[0, 0].start()
    copies[1, 0].start()
    copies[2, 0].start()
    copies[3, 0].start()
    copies[0, 1].start()
    copies[1, 1].start()
    copies[2, 1].start()
    copies[3, 1].start()
    copies[2, 2].start()
    copies[3, 2].start()
    copies[2, 3].start()
    copies[3, 3].start()
    fetch.start()
    rows, cols = rows_ref[...], cols_ref[...]
    build_forward(sizes, rows, cols, fwd_high, fwd_low)
    build_bands(depth_ref[...].astype(jnp.float32), band, band_t)
    build_backward(sizes, rows, cols, bwd_high, bwd_low)
    home.wait()
    relay(0)
    copies[0, 2].start()
    copies[1, 2].start()
    middle(0, 2)
    relay(1)
    copies[0, 3].start()
    copies[1, 3].start()
    middle(2, 4)
    edges(0, 2)
    fetch.wait()
    relay(2)
    along_depth(0)
    gradient(0)
    against_depth(0)
    corners(0, 1)
    relay(3)
    edges(2, 3)
    along_depth(1)
    gradient(1)
    against_depth(1)
    corners(1, 2)
    strips(0)
    edges(3, 4)
    along_depth(2)
    gradient(2)
    against_depth(2)
    corners(2, 4)
    strips(1)
    sides(0, 4)
    strips(2)
    strips(3)
    outs = [final(c) for c in range(chunks)]
    for copy in list(copies.values()) + list(returns.values()):
        copy.wait_send()


def per_device(tangent, hessian, kernel_rows, kernel_cols, kernel_depth):
    span_rows, span_cols, depth = tangent.shape
    reach = RADIUS
    ext_rows, ext_cols = span_rows + 2 * reach, span_cols + 2 * reach
    sizes = (span_rows, span_cols, ext_rows, ext_cols)
    counts = (lax.axis_size("gx"), lax.axis_size("gy"))
    own, wide = span_rows * span_cols, ext_rows * ext_cols
    groups, size, block = span_rows // reach, reach * span_cols, reach * ext_cols
    chunks = depth // LANES
    full = pl.BlockSpec(memory_space=pltpu.VMEM)
    anywhere = pl.BlockSpec(memory_space=pl.ANY)
    bf16, f32 = jnp.bfloat16, jnp.float32
    return pl.pallas_call(
        lambda *refs: compute(sizes, counts, *refs),
        out_shape=pltpu.VMEM((span_rows, span_cols, depth), f32),
        in_specs=[anywhere, anywhere, full, full, full],
        out_specs=full,
        scratch_shapes=[
            pltpu.VMEM((ext_rows, ext_cols, depth), f32),
            pltpu.VMEM((wide, depth), bf16),
            pltpu.VMEM((wide, depth), bf16),
            pltpu.VMEM((DENSITIES * size, 3 * block), bf16),
            pltpu.VMEM((DENSITIES * size, 3 * block), bf16),
            pltpu.VMEM((3 * block, DENSITIES * size), bf16),
            pltpu.VMEM((3 * block, DENSITIES * size), bf16),
            pltpu.VMEM((DENSITIES, WINDOW, WINDOW), bf16),
            pltpu.VMEM((DENSITIES, WINDOW, WINDOW), bf16),
            pltpu.VMEM((DENSITIES, DENSITIES, own, depth), bf16),
            pltpu.VMEM((groups, DENSITIES * size, depth), f32),
            pltpu.VMEM((DENSITIES, own, depth), bf16),
            pltpu.VMEM((DENSITIES, own, depth), f32),
            pltpu.VMEM((DENSITIES, own, depth), bf16),
            pltpu.VMEM((DENSITIES, own, LANES), f32),
            pltpu.VMEM((groups, DENSITIES * size, depth), bf16),
            pltpu.VMEM((groups, DENSITIES * size, depth), bf16),
            pltpu.VMEM((ext_rows, ext_cols, depth), f32),
            pltpu.VMEM((ext_rows, reach, depth), f32),
            pltpu.VMEM((ext_rows, reach, depth), f32),
            pltpu.VMEM((reach, span_cols, depth), f32),
            pltpu.VMEM((reach, span_cols, depth), f32),
            pltpu.SemaphoreType.DMA((2,)),
            pltpu.SemaphoreType.DMA((chunks,)),
            pltpu.SemaphoreType.DMA((8, chunks)),
            pltpu.SemaphoreType.DMA((8, chunks)),
            pltpu.SemaphoreType.DMA((8, chunks)),
            pltpu.SemaphoreType.DMA((8, chunks)),
        ],
        compiler_params=pltpu.CompilerParams(
            vmem_limit_bytes=60 << 20, collective_id=0, has_side_effects=True),
    )(tangent, hessian.reshape(DENSITIES, DENSITIES, own, depth), kernel_rows, kernel_cols, kernel_depth)


def solution(mesh):
    return jax.shard_map(
        per_device,
        mesh=mesh,
        in_specs=(P("gx", "gy", None), P(None, None, "gx", "gy", None), P(), P(), P()),
        out_specs=P("gx", "gy", None),
        check_vma=False,
    )
```

```python
import jax
import jax.numpy as jnp
from jax import lax
from jax.experimental import pallas as pl
from jax.experimental.pallas import tpu as pltpu
from jax.sharding import PartitionSpec as P

RADIUS = 8
DENSITIES = 5
TAPS = 2 * RADIUS + 1
LANES = 128
WINDOW = 2 * LANES


def split(value):
    high = value.astype(jnp.bfloat16)
    low = (value - high.astype(jnp.float32)).astype(jnp.bfloat16)
    return high, low


def dot(left, right):
    return jnp.dot(left, right, preferred_element_type=jnp.float32)


def dot3(left_high, left_low, right_high, right_low):
    return dot(left_high, right_high) + dot(left_high, right_low) + dot(left_low, right_high)


def picked(taps, index):
    total = jnp.zeros(index.shape, jnp.float32)
    for tap in range(TAPS):
        weight = jnp.broadcast_to(taps[:, tap : tap + 1], index.shape)
        total = jnp.where(index == tap, weight, total)
    return total


def iota(shape, axis):
    return lax.broadcasted_iota(jnp.int32, shape, axis)


def build_forward(sizes, rows, cols, high_ref, low_ref):
    span_cols, ext_cols = sizes[1], sizes[3]
    wide = 3 * RADIUS * ext_cols
    row_index = iota((RADIUS, wide), 1) // ext_cols - iota((RADIUS, wide), 0)
    col_index = iota((span_cols, LANES), 1) % ext_cols - iota((span_cols, LANES), 0)
    for a in range(DENSITIES):
        by_row = picked(rows[a : a + 1], row_index)
        by_col = picked(cols[a : a + 1], col_index)
        by_col = jnp.concatenate([by_col] * (wide // LANES), axis=1)
        for r in range(RADIUS):
            at = pl.ds((a * RADIUS + r) * span_cols, span_cols)
            high_ref[at, :], low_ref[at, :] = split(by_row[r : r + 1, :] * by_col)


def build_backward(sizes, rows, cols, high_ref, low_ref):
    span_cols, ext_cols = sizes[1], sizes[3]
    size = RADIUS * span_cols
    row_index = iota((3 * RADIUS, size), 0) - iota((3 * RADIUS, size), 1) // span_cols
    col_index = iota((ext_cols, size), 0) - iota((ext_cols, size), 1) % span_cols
    for a in range(DENSITIES):
        by_row = picked(rows[a : a + 1], row_index)
        by_col = picked(cols[a : a + 1], col_index)
        into = pl.ds(a * size, size)
        for r in range(3 * RADIUS):
            at = pl.ds(r * ext_cols, ext_cols)
            high_ref[at, into], low_ref[at, into] = split(by_row[r : r + 1, :] * by_col)


def build_bands(depth_taps, band_ref, band_t_ref):
    step = 16
    shape = (step, WINDOW)
    offset = iota(shape, 0) - iota(shape, 1)
    for a in range(DENSITIES):
        taps = depth_taps[a : a + 1]
        for ref, sign in ((band_ref, 1), (band_t_ref, -1)):
            middle = picked(taps, sign * (offset + LANES) + RADIUS)
            for i in range(WINDOW // step):
                value = pltpu.roll(middle, (step * i - LANES) % WINDOW, 1)
                if i in (0, WINDOW // step - 1):
                    value = jnp.where(jnp.abs(offset + step * i) <= RADIUS, value, 0.0)
                ref[a, pl.ds(i * step, step), :] = value.astype(jnp.bfloat16)


def compute(sizes, counts, tangent_ref, hess_ref, rows_ref, cols_ref, depth_ref, out_ref,
            ext, high, low, fwd_high, fwd_low, bwd_high, bwd_low, band, band_t, hess,
            acc, lateral, dens, lowered, pending, back_high, back_low, spread,
            from_left, from_right, from_ring,
            local_sems, send_sems, recv_sems, back_send_sems, back_recv_sems):
    span_rows, span_cols, ext_rows, ext_cols = sizes
    depth = acc.shape[-1]
    reach = RADIUS
    groups = span_rows // reach
    own, size, block = span_rows * span_cols, reach * span_cols, reach * ext_cols
    chunks = depth // LANES
    gx, gy = lax.axis_index("gx"), lax.axis_index("gy")
    left = {"gy": lax.rem(gy + counts[1] - 1, counts[1])}
    right = {"gy": lax.rem(gy + 1, counts[1])}
    mesh_ids = pl.DeviceIdType.MESH

    inner_rows, inner_cols = pl.ds(reach, span_rows), pl.ds(reach, span_cols)
    barrier = pltpu.get_barrier_semaphore()
    rings = [{"gx": lax.rem(gx + counts[0] + step, counts[0])} for step in (-1, 1)]
    for neighbour in (*rings, left, right):
        pl.semaphore_signal(barrier, inc=1, device_id=neighbour, device_id_type=mesh_ids)
    fetch = pltpu.make_async_copy(hess_ref, hess, local_sems.at[0])
    home = pltpu.make_async_copy(tangent_ref, ext.at[inner_rows, inner_cols, :], local_sems.at[1])
    home.start()
    pl.semaphore_wait(barrier, 4)

    first_cols, last_cols = pl.ds(0, reach), pl.ds(reach + span_cols, reach)
    near_first, near_last = pl.ds(reach, reach), pl.ds(span_cols, reach)
    lanes = [pl.ds(c * LANES, LANES) for c in range(chunks)]

    def remote(source, target, send_sem, recv_sem, device):
        return pltpu.make_async_remote_copy(
            src_ref=source, dst_ref=target, send_sem=send_sem, recv_sem=recv_sem,
            device_id=device, device_id_type=mesh_ids)

    head_cols, tail_cols = pl.ds(0, reach), pl.ds(span_cols - reach, reach)
    every_row, every_col = pl.ds(0, span_rows), pl.ds(0, span_cols)
    copies, returns = {}, {}
    for c, z in enumerate(lanes):
        plan = [
            (tangent_ref.at[every_row, tail_cols, z], ext.at[inner_rows, first_cols, z], right),
            (tangent_ref.at[every_row, head_cols, z], ext.at[inner_rows, last_cols, z], left),
        ]
        for side, (source, target, device) in enumerate(plan):
            copies[2 + side, c] = remote(source, target, send_sems.at[2 + side, c], recv_sems.at[2 + side, c], device)
        plan = [
            (spread.at[inner_rows, last_cols, z], from_left.at[inner_rows, :, z], right),
            (spread.at[inner_rows, first_cols, z], from_right.at[inner_rows, :, z], left),
        ]
        for side, (source, target, device) in enumerate(plan):
            returns[4 + side, c] = remote(source, target, back_send_sems.at[4 + side, c], back_recv_sems.at[4 + side, c], device)

    odd = lax.rem(gx, 2)
    FAR, NEAR = odd, 1 - odd

    def ring(group):
        return {"gx": lax.rem(gx + counts[0] - 1 + 2 * group, counts[0])}

    def halo(group):
        return pl.ds(group * (reach + span_rows), reach)

    def halo_copy(group, c):
        z = lanes[c]
        source = tangent_ref.at[pl.ds(group * (span_rows - reach), reach), every_col, z]
        return remote(source, ext.at[halo(1 - group), inner_cols, z], send_sems.at[1 - group, c], recv_sems.at[1 - group, c], ring(group))

    def corner_copies(group, c):
        z, rows_at = lanes[c], halo(group)
        for side, near, far, device in ((0, near_last, first_cols, right), (1, near_first, last_cols, left)):
            kind = 4 + 2 * group + side
            yield remote(ext.at[rows_at, near, z], ext.at[rows_at, far, z], send_sems.at[kind, c], recv_sems.at[kind, c], device)

    def return_copies(group, c):
        z, rows_at = lanes[c], halo(group)
        for side, cols_at, target, device in ((0, last_cols, from_left, right), (1, first_cols, from_right, left)):
            kind = 2 * group + side
            yield remote(spread.at[rows_at, cols_at, z], target.at[rows_at, :, z], back_send_sems.at[kind, c], back_recv_sems.at[kind, c], device)

    def strip_copy(group, c):
        z, kind = lanes[c], 6 + group
        return remote(spread.at[halo(group), inner_cols, z], from_ring.at[1 - group, :, :, z], back_send_sems.at[kind, c], back_recv_sems.at[kind, c], ring(group))

    def launch(*pairs):
        for kind, c in pairs:
            copies[kind, c].start()

    def relay(group, c):
        halo_copy(1 - group, c).wait_recv()
        for copy in corner_copies(group, c):
            copy.start()

    def at_lanes(begin, end):
        return pl.ds(begin * LANES, (end - begin) * LANES)

    def prepare(z, start, count):
        value = ext[pl.ds(start, count), :, z].reshape(count * ext_cols, z.size)
        at = pl.ds(start * ext_cols, count * ext_cols)
        high[at, z], low[at, z] = split(value)

    def middle(begin, end):
        z = at_lanes(begin, end)
        for c in range(begin, end):
            copies[2, c].wait_recv()
            copies[3, c].wait_recv()
        prepare(z, reach, span_rows)
        data = pl.ds(block, 2 * block)
        for group in (0, 1):
            weights = pl.ds((1 - group) * block, 2 * block)
            acc[group, :, z] = dot3(fwd_high[:, weights], fwd_low[:, weights], high[data, z], low[data, z])

    def arrived(group, begin, end):
        for c in range(begin, end):
            for copy in corner_copies(group, c):
                copy.wait_recv()

    def edges(group, begin, end):
        def emit():
            z = at_lanes(begin, end)
            prepare(z, group * (reach + span_rows), reach)
            weights, data = pl.ds(group * 2 * block, block), pl.ds(group * 3 * block, block)
            total = acc[group, :, z] + dot3(fwd_high[:, weights], fwd_low[:, weights], high[data, z], low[data, z])
            lateral[group, :, z] = total.astype(jnp.bfloat16)

        return [emit]

    keep = iota((size, LANES), 1) < LANES // 2

    def along_depth(group, k):
        z, here, ahead = pl.ds(k * LANES, WINDOW), lanes[k], lanes[k + 1]

        def emit(a):
            part = pl.ds(a * size, size)
            value = dot(lateral[group, part, z], band[a])
            begin = value[:, :LANES]
            dens[group, part, here] = begin if k == 0 else jnp.where(keep, dens[group, part, here], begin)
            dens[group, part, ahead] = value[:, LANES:]

        return [lambda a=a: emit(a) for a in range(DENSITIES)]

    def gradient(group, k):
        step = 16

        def emit(r, z):
            at = pl.ds(group * size + r * step, step)
            values = [dens[group, pl.ds(b * size + r * step, step), z] for b in range(DENSITIES)]
            for a in range(DENSITIES):
                total = None
                for b in range(DENSITIES):
                    term = hess[a, b, at, z].astype(jnp.float32) * values[b]
                    total = term if total is None else total + term
                lowered[group, pl.ds(a * size + r * step, step), z] = total.astype(jnp.bfloat16)

        return [lambda r=r, z=z: emit(r, z) for r in range(size // step) for z in (lanes[k], lanes[k + 1])]

    def against_depth(group, k):
        z, here, ahead = pl.ds(k * LANES, WINDOW), lanes[k], lanes[k + 1]

        def emit(a):
            part = pl.ds(a * size, size)
            value = dot(lowered[group, part, z], band_t[a])
            begin, rest = value[:, :LANES], value[:, LANES:]
            if k > 0:
                begin = jnp.where(keep, pending[group, part, :], begin)
            back_high[group, part, here], back_low[group, part, here] = split(begin)
            if k == chunks - 2:
                back_high[group, part, ahead], back_low[group, part, ahead] = split(rest)
            else:
                pending[group, part, :] = rest

        return [lambda a=a: emit(a) for a in range(DENSITIES)]

    def corners(group, begin, end):
        def emit():
            z = at_lanes(begin, end)
            part = pl.ds(group * 2 * block, block)
            value = dot3(bwd_high[part, :], bwd_low[part, :], back_high[group, :, z], back_low[group, :, z])
            spread[halo(group), :, z] = value.reshape(reach, ext_cols, z.size)

        return [emit]

    def send_corners(group, begin, end):
        for c in range(begin, end):
            for copy in return_copies(group, c):
                copy.start()

    def sides(begin, end):
        z = at_lanes(begin, end)
        for index in (0, 1):
            total = None
            for group in (0, 1):
                part = pl.ds((1 + index - group) * block, block)
                term = dot3(bwd_high[part, :], bwd_low[part, :], back_high[group, :, z], back_low[group, :, z])
                total = term if total is None else total + term
            spread[pl.ds((1 + index) * reach, reach), :, z] = total.reshape(reach, ext_cols, z.size)
        for c in range(begin, end):
            for kind in (4, 5):
                returns[kind, c].start()

    def strips(group, c):
        z, rows_at = lanes[c], halo(group)
        for copy in return_copies(group, c):
            copy.wait_recv()
        spread[rows_at, near_first, z] = spread[rows_at, near_first, z] + from_left[rows_at, :, z]
        spread[rows_at, near_last, z] = spread[rows_at, near_last, z] + from_right[rows_at, :, z]
        strip_copy(group, c).start()

    def final(c):
        z = lanes[c]
        for kind in (4, 5):
            returns[kind, c].wait_recv()
        spread[inner_rows, near_first, z] = spread[inner_rows, near_first, z] + from_left[inner_rows, :, z]
        spread[inner_rows, near_last, z] = spread[inner_rows, near_last, z] + from_right[inner_rows, :, z]
        for group in (0, 1):
            strip_copy(1 - group, c).wait_recv()
            edge, rows_at = pl.ds(reach + group * reach, reach), pl.ds(group * reach, reach)
            out_ref[rows_at, :, z] = spread[edge, inner_cols, z] + from_ring[group, :, :, z]

    def mix(*streams):
        order = sorted(((n + 0.5) / len(stream), m, n) for m, stream in enumerate(streams) for n in range(len(stream)))
        for _, m, n in order:
            streams[m][n]()

    halo_copy(FAR, 0).start()
    halo_copy(NEAR, 0).start()
    launch((2, 0), (3, 0))
    halo_copy(FAR, 1).start()
    halo_copy(NEAR, 1).start()
    launch((2, 1), (3, 1))
    launch((2, 2), (3, 2))
    launch((2, 3), (3, 3))
    fetch.start()
    rows, cols = rows_ref[...], cols_ref[...]
    build_forward(sizes, rows, cols, fwd_high, fwd_low)
    build_bands(depth_ref[...].astype(jnp.float32), band, band_t)
    build_backward(sizes, rows, cols, bwd_high, bwd_low)
    home.wait()
    relay(FAR, 0)
    relay(NEAR, 0)
    halo_copy(FAR, 2).start()
    halo_copy(NEAR, 2).start()
    middle(0, 2)
    relay(FAR, 1)
    relay(NEAR, 1)
    halo_copy(FAR, 3).start()
    halo_copy(NEAR, 3).start()
    middle(2, 4)
    fetch.wait()
    arrived(FAR, 0, 2)
    arrived(NEAR, 0, 2)
    mix(edges(0, 0, 2))
    mix(edges(1, 0, 2))
    relay(FAR, 2)
    relay(NEAR, 2)
    mix(along_depth(0, 0))
    mix(along_depth(1, 0))
    mix(gradient(0, 0))
    mix(gradient(1, 0))
    mix(against_depth(0, 0))
    mix(against_depth(1, 0))
    mix(corners(0, 0, 1))
    mix(corners(1, 0, 1))
    send_corners(FAR, 0, 1)
    send_corners(NEAR, 0, 1)
    relay(FAR, 3)
    relay(NEAR, 3)
    arrived(FAR, 2, 3)
    arrived(NEAR, 2, 3)
    mix(edges(0, 2, 3))
    mix(edges(1, 2, 3))
    mix(along_depth(0, 1))
    mix(along_depth(1, 1))
    mix(gradient(0, 1))
    mix(gradient(1, 1))
    mix(against_depth(0, 1))
    mix(against_depth(1, 1))
    mix(corners(0, 1, 2))
    mix(corners(1, 1, 2))
    send_corners(FAR, 1, 2)
    send_corners(NEAR, 1, 2)
    strips(FAR, 0)
    strips(NEAR, 0)
    arrived(FAR, 3, 4)
    arrived(NEAR, 3, 4)
    mix(edges(0, 3, 4))
    mix(edges(1, 3, 4))
    mix(along_depth(0, 2))
    mix(along_depth(1, 2))
    mix(gradient(0, 2))
    mix(gradient(1, 2))
    mix(against_depth(0, 2))
    mix(against_depth(1, 2))
    mix(corners(0, 2, 4))
    mix(corners(1, 2, 4))
    send_corners(FAR, 2, 4)
    send_corners(NEAR, 2, 4)
    strips(FAR, 1)
    strips(NEAR, 1)
    sides(0, 2)
    strips(FAR, 2)
    strips(NEAR, 2)
    strips(FAR, 3)
    strips(NEAR, 3)
    sides(2, 4)
    final(0)
    final(1)
    final(2)
    final(3)
    for copy in list(copies.values()) + list(returns.values()):
        copy.wait_send()
    for c in range(chunks):
        for group in (0, 1):
            halo_copy(group, c).wait_send()
            strip_copy(group, c).wait_send()
            for copy in (*corner_copies(group, c), *return_copies(group, c)):
                copy.wait_send()


def per_device(tangent, hessian, kernel_rows, kernel_cols, kernel_depth):
    span_rows, span_cols, depth = tangent.shape
    reach = RADIUS
    ext_rows, ext_cols = span_rows + 2 * reach, span_cols + 2 * reach
    sizes = (span_rows, span_cols, ext_rows, ext_cols)
    counts = (lax.axis_size("gx"), lax.axis_size("gy"))
    own, wide = span_rows * span_cols, ext_rows * ext_cols
    groups, size, block = span_rows // reach, reach * span_cols, reach * ext_cols
    chunks = depth // LANES
    assert groups == 2 and chunks > 1 and counts[0] % 2 == 0
    full = pl.BlockSpec(memory_space=pltpu.VMEM)
    anywhere = pl.BlockSpec(memory_space=pl.ANY)
    bf16, f32 = jnp.bfloat16, jnp.float32
    return pl.pallas_call(
        lambda *refs: compute(sizes, counts, *refs),
        out_shape=pltpu.VMEM((span_rows, span_cols, depth), f32),
        in_specs=[anywhere, anywhere, full, full, full],
        out_specs=full,
        scratch_shapes=[
            pltpu.VMEM((ext_rows, ext_cols, depth), f32),
            pltpu.VMEM((wide, depth), bf16),
            pltpu.VMEM((wide, depth), bf16),
            pltpu.VMEM((DENSITIES * size, 3 * block), bf16),
            pltpu.VMEM((DENSITIES * size, 3 * block), bf16),
            pltpu.VMEM((3 * block, DENSITIES * size), bf16),
            pltpu.VMEM((3 * block, DENSITIES * size), bf16),
            pltpu.VMEM((DENSITIES, WINDOW, WINDOW), bf16),
            pltpu.VMEM((DENSITIES, WINDOW, WINDOW), bf16),
            pltpu.VMEM((DENSITIES, DENSITIES, own, depth), bf16),
            pltpu.VMEM((groups, DENSITIES * size, depth), f32),
            pltpu.VMEM((groups, DENSITIES * size, depth), bf16),
            pltpu.VMEM((groups, DENSITIES * size, depth), f32),
            pltpu.VMEM((groups, DENSITIES * size, depth), bf16),
            pltpu.VMEM((groups, DENSITIES * size, LANES), f32),
            pltpu.VMEM((groups, DENSITIES * size, depth), bf16),
            pltpu.VMEM((groups, DENSITIES * size, depth), bf16),
            pltpu.VMEM((ext_rows, ext_cols, depth), f32),
            pltpu.VMEM((ext_rows, reach, depth), f32),
            pltpu.VMEM((ext_rows, reach, depth), f32),
            pltpu.VMEM((2, reach, span_cols, depth), f32),
            pltpu.SemaphoreType.DMA((2,)),
            pltpu.SemaphoreType.DMA((8, chunks)),
            pltpu.SemaphoreType.DMA((8, chunks)),
            pltpu.SemaphoreType.DMA((8, chunks)),
            pltpu.SemaphoreType.DMA((8, chunks)),
        ],
        compiler_params=pltpu.CompilerParams(
            vmem_limit_bytes=60 << 20, collective_id=0, has_side_effects=True),
    )(tangent, hessian.reshape(DENSITIES, DENSITIES, own, depth), kernel_rows, kernel_cols, kernel_depth)


def solution(mesh):
    return jax.shard_map(
        per_device,
        mesh=mesh,
        in_specs=(P("gx", "gy", None), P(None, None, "gx", "gy", None), P(), P(), P()),
        out_specs=P("gx", "gy", None),
        check_vma=False,
    )
```

```python
import jax
import jax.numpy as jnp
from jax import lax
from jax.experimental import pallas as pl
from jax.experimental.pallas import tpu as pltpu
from jax.sharding import PartitionSpec as P

RADIUS = 8
DENSITIES = 5
TAPS = 2 * RADIUS + 1
LANES = 128
WINDOW = 2 * LANES


def split(value):
    high = value.astype(jnp.bfloat16)
    low = (value - high.astype(jnp.float32)).astype(jnp.bfloat16)
    return high, low


def dot(left, right):
    return jnp.dot(left, right, preferred_element_type=jnp.float32)


def dot3(left_high, left_low, right_high, right_low):
    return dot(left_high, right_high) + dot(left_high, right_low) + dot(left_low, right_high)


def picked(taps, index):
    total = jnp.zeros(index.shape, jnp.float32)
    for tap in range(TAPS):
        weight = jnp.broadcast_to(taps[:, tap : tap + 1], index.shape)
        total = jnp.where(index == tap, weight, total)
    return total


def iota(shape, axis):
    return lax.broadcasted_iota(jnp.int32, shape, axis)


def build_forward(sizes, rows, cols, high_ref, low_ref):
    span_cols, ext_cols = sizes[1], sizes[3]
    wide = 3 * RADIUS * ext_cols
    row_index = iota((RADIUS, wide), 1) // ext_cols - iota((RADIUS, wide), 0)
    col_index = iota((span_cols, LANES), 1) % ext_cols - iota((span_cols, LANES), 0)
    for a in range(DENSITIES):
        by_row = picked(rows[a : a + 1], row_index)
        by_col = picked(cols[a : a + 1], col_index)
        by_col = jnp.concatenate([by_col] * (wide // LANES), axis=1)
        for r in range(RADIUS):
            at = pl.ds((a * RADIUS + r) * span_cols, span_cols)
            high_ref[at, :], low_ref[at, :] = split(by_row[r : r + 1, :] * by_col)


def build_backward(sizes, rows, cols, high_ref, low_ref):
    span_cols, ext_cols = sizes[1], sizes[3]
    size = RADIUS * span_cols
    row_index = iota((3 * RADIUS, size), 0) - iota((3 * RADIUS, size), 1) // span_cols
    col_index = iota((ext_cols, size), 0) - iota((ext_cols, size), 1) % span_cols
    for a in range(DENSITIES):
        by_row = picked(rows[a : a + 1], row_index)
        by_col = picked(cols[a : a + 1], col_index)
        into = pl.ds(a * size, size)
        for r in range(3 * RADIUS):
            at = pl.ds(r * ext_cols, ext_cols)
            high_ref[at, into], low_ref[at, into] = split(by_row[r : r + 1, :] * by_col)


def build_bands(depth_taps, band_ref, band_t_ref):
    step = 16
    shape = (step, WINDOW)
    offset = iota(shape, 0) - iota(shape, 1)
    for a in range(DENSITIES):
        taps = depth_taps[a : a + 1]
        for ref, sign in ((band_ref, 1), (band_t_ref, -1)):
            middle = picked(taps, sign * (offset + LANES) + RADIUS)
            for i in range(WINDOW // step):
                value = pltpu.roll(middle, (step * i - LANES) % WINDOW, 1)
                if i in (0, WINDOW // step - 1):
                    value = jnp.where(jnp.abs(offset + step * i) <= RADIUS, value, 0.0)
                ref[a, pl.ds(i * step, step), :] = value.astype(jnp.bfloat16)


def compute(sizes, counts, tangent_ref, hess_ref, rows_hbm, cols_hbm, depth_hbm, out_ref,
            ext, high, low, fwd_high, fwd_low, bwd_high, bwd_low, band, band_t, hess,
            acc, lateral, dens, lowered, pending, back_high, back_low, spread,
            from_left, from_right, from_ring, rows_ref, cols_ref, depth_ref,
            local_sems, send_sems, recv_sems, back_send_sems, back_recv_sems):
    span_rows, span_cols, ext_rows, ext_cols = sizes
    depth = acc.shape[-1]
    reach = RADIUS
    groups = span_rows // reach
    own, size, block = span_rows * span_cols, reach * span_cols, reach * ext_cols
    chunks = depth // LANES
    gx, gy = lax.axis_index("gx"), lax.axis_index("gy")
    left = {"gy": lax.rem(gy + counts[1] - 1, counts[1])}
    right = {"gy": lax.rem(gy + 1, counts[1])}
    mesh_ids = pl.DeviceIdType.MESH

    inner_rows, inner_cols = pl.ds(reach, span_rows), pl.ds(reach, span_cols)
    barrier = pltpu.get_barrier_semaphore()
    rings = [{"gx": lax.rem(gx + counts[0] + step, counts[0])} for step in (-1, 1)]
    for neighbour in (*rings, left, right):
        pl.semaphore_signal(barrier, inc=1, device_id=neighbour, device_id_type=mesh_ids)
    fetch = pltpu.make_async_copy(hess_ref, hess, local_sems.at[0])
    home = pltpu.make_async_copy(tangent_ref, ext.at[inner_rows, inner_cols, :], local_sems.at[1])
    home.start()
    factors = [pltpu.make_async_copy(source, target, local_sems.at[2 + n]) for n, (source, target) in enumerate(
        ((rows_hbm, rows_ref), (cols_hbm, cols_ref), (depth_hbm, depth_ref)))]
    for copy in factors:
        copy.start()
    pl.semaphore_wait(barrier, 4)

    first_cols, last_cols = pl.ds(0, reach), pl.ds(reach + span_cols, reach)
    near_first, near_last = pl.ds(reach, reach), pl.ds(span_cols, reach)
    lanes = [pl.ds(c * LANES, LANES) for c in range(chunks)]

    def remote(source, target, send_sem, recv_sem, device):
        return pltpu.make_async_remote_copy(
            src_ref=source, dst_ref=target, send_sem=send_sem, recv_sem=recv_sem,
            device_id=device, device_id_type=mesh_ids)

    head_cols, tail_cols = pl.ds(0, reach), pl.ds(span_cols - reach, reach)
    every_row, every_col = pl.ds(0, span_rows), pl.ds(0, span_cols)
    copies, returns = {}, {}
    for c, z in enumerate(lanes):
        plan = [
            (tangent_ref.at[every_row, tail_cols, z], ext.at[inner_rows, first_cols, z], right),
            (tangent_ref.at[every_row, head_cols, z], ext.at[inner_rows, last_cols, z], left),
        ]
        for side, (source, target, device) in enumerate(plan):
            copies[2 + side, c] = remote(source, target, send_sems.at[2 + side, c], recv_sems.at[2 + side, c], device)
        plan = [
            (spread.at[inner_rows, last_cols, z], from_left.at[inner_rows, :, z], right),
            (spread.at[inner_rows, first_cols, z], from_right.at[inner_rows, :, z], left),
        ]
        for side, (source, target, device) in enumerate(plan):
            returns[4 + side, c] = remote(source, target, back_send_sems.at[4 + side, c], back_recv_sems.at[4 + side, c], device)

    odd = lax.rem(gx, 2)
    FAR, NEAR = odd, 1 - odd

    def ring(group):
        return {"gx": lax.rem(gx + counts[0] - 1 + 2 * group, counts[0])}

    def halo(group):
        return pl.ds(group * (reach + span_rows), reach)

    def halo_copy(group, c):
        z = lanes[c]
        source = tangent_ref.at[pl.ds(group * (span_rows - reach), reach), every_col, z]
        return remote(source, ext.at[halo(1 - group), inner_cols, z], send_sems.at[1 - group, c], recv_sems.at[1 - group, c], ring(group))

    def corner_copies(group, c):
        z, rows_at = lanes[c], halo(group)
        for side, near, far, device in ((0, near_last, first_cols, right), (1, near_first, last_cols, left)):
            kind = 4 + 2 * group + side
            yield remote(ext.at[rows_at, near, z], ext.at[rows_at, far, z], send_sems.at[kind, c], recv_sems.at[kind, c], device)

    def return_copies(group, c):
        z, rows_at = lanes[c], halo(group)
        for side, cols_at, target, device in ((0, last_cols, from_left, right), (1, first_cols, from_right, left)):
            kind = 2 * group + side
            yield remote(spread.at[rows_at, cols_at, z], target.at[rows_at, :, z], back_send_sems.at[kind, c], back_recv_sems.at[kind, c], device)

    def strip_copy(group, c):
        z, kind = lanes[c], 6 + group
        return remote(spread.at[halo(group), inner_cols, z], from_ring.at[1 - group, :, :, z], back_send_sems.at[kind, c], back_recv_sems.at[kind, c], ring(group))

    def launch(*pairs):
        for kind, c in pairs:
            copies[kind, c].start()

    def relay(group, c):
        halo_copy(1 - group, c).wait_recv()
        for copy in corner_copies(group, c):
            copy.start()

    def at_lanes(begin, end):
        return pl.ds(begin * LANES, (end - begin) * LANES)

    def prepare(z, start, count):
        value = ext[pl.ds(start, count), :, z].reshape(count * ext_cols, z.size)
        at = pl.ds(start * ext_cols, count * ext_cols)
        high[at, z], low[at, z] = split(value)

    def middle(begin, end):
        z = at_lanes(begin, end)
        for c in range(begin, end):
            copies[2, c].wait_recv()
            copies[3, c].wait_recv()
        prepare(z, reach, span_rows)
        data = pl.ds(block, 2 * block)
        for group in (0, 1):
            weights = pl.ds((1 - group) * block, 2 * block)
            acc[group, :, z] = dot3(fwd_high[:, weights], fwd_low[:, weights], high[data, z], low[data, z])

    def arrived(group, begin, end):
        for c in range(begin, end):
            for copy in corner_copies(group, c):
                copy.wait_recv()

    def edges(group, begin, end):
        def emit():
            z = at_lanes(begin, end)
            prepare(z, group * (reach + span_rows), reach)
            weights, data = pl.ds(group * 2 * block, block), pl.ds(group * 3 * block, block)
            total = acc[group, :, z] + dot3(fwd_high[:, weights], fwd_low[:, weights], high[data, z], low[data, z])
            lateral[group, :, z] = total.astype(jnp.bfloat16)

        return [emit]

    keep = iota((size, LANES), 1) < LANES // 2

    def along_depth(group, k):
        z, here, ahead = pl.ds(k * LANES, WINDOW), lanes[k], lanes[k + 1]

        def emit(a):
            part = pl.ds(a * size, size)
            value = dot(lateral[group, part, z], band[a])
            begin = value[:, :LANES]
            dens[group, part, here] = begin if k == 0 else jnp.where(keep, dens[group, part, here], begin)
            dens[group, part, ahead] = value[:, LANES:]

        return [lambda a=a: emit(a) for a in range(DENSITIES)]

    def gradient(group, k):
        step = 16

        def emit(r, z):
            at = pl.ds(group * size + r * step, step)
            values = [dens[group, pl.ds(b * size + r * step, step), z] for b in range(DENSITIES)]
            for a in range(DENSITIES):
                total = None
                for b in range(DENSITIES):
                    term = hess[a, b, at, z].astype(jnp.float32) * values[b]
                    total = term if total is None else total + term
                lowered[group, pl.ds(a * size + r * step, step), z] = total.astype(jnp.bfloat16)

        return [lambda r=r, z=z: emit(r, z) for r in range(size // step) for z in (lanes[k], lanes[k + 1])]

    def against_depth(group, k):
        z, here, ahead = pl.ds(k * LANES, WINDOW), lanes[k], lanes[k + 1]

        def emit(a):
            part = pl.ds(a * size, size)
            value = dot(lowered[group, part, z], band_t[a])
            begin, rest = value[:, :LANES], value[:, LANES:]
            if k > 0:
                begin = jnp.where(keep, pending[group, part, :], begin)
            back_high[group, part, here], back_low[group, part, here] = split(begin)
            if k == chunks - 2:
                back_high[group, part, ahead], back_low[group, part, ahead] = split(rest)
            else:
                pending[group, part, :] = rest

        return [lambda a=a: emit(a) for a in range(DENSITIES)]

    def corners(group, begin, end):
        def emit():
            z = at_lanes(begin, end)
            part = pl.ds(group * 2 * block, block)
            value = dot3(bwd_high[part, :], bwd_low[part, :], back_high[group, :, z], back_low[group, :, z])
            spread[halo(group), :, z] = value.reshape(reach, ext_cols, z.size)

        return [emit]

    def send_corners(group, begin, end):
        for c in range(begin, end):
            for copy in return_copies(group, c):
                copy.start()

    def sides(begin, end):
        z = at_lanes(begin, end)
        for index in (0, 1):
            total = None
            for group in (0, 1):
                part = pl.ds((1 + index - group) * block, block)
                term = dot3(bwd_high[part, :], bwd_low[part, :], back_high[group, :, z], back_low[group, :, z])
                total = term if total is None else total + term
            spread[pl.ds((1 + index) * reach, reach), :, z] = total.reshape(reach, ext_cols, z.size)
        for c in range(begin, end):
            for kind in (4, 5):
                returns[kind, c].start()

    def strips(group, c):
        z, rows_at = lanes[c], halo(group)
        for copy in return_copies(group, c):
            copy.wait_recv()
        spread[rows_at, near_first, z] = spread[rows_at, near_first, z] + from_left[rows_at, :, z]
        spread[rows_at, near_last, z] = spread[rows_at, near_last, z] + from_right[rows_at, :, z]
        strip_copy(group, c).start()

    def final(c):
        z = lanes[c]
        for kind in (4, 5):
            returns[kind, c].wait_recv()
        spread[inner_rows, near_first, z] = spread[inner_rows, near_first, z] + from_left[inner_rows, :, z]
        spread[inner_rows, near_last, z] = spread[inner_rows, near_last, z] + from_right[inner_rows, :, z]
        for group in (0, 1):
            strip_copy(1 - group, c).wait_recv()
            edge, rows_at = pl.ds(reach + group * reach, reach), pl.ds(group * reach, reach)
            out_ref[rows_at, :, z] = spread[edge, inner_cols, z] + from_ring[group, :, :, z]

    def mix(*streams):
        order = sorted(((n + 0.5) / len(stream), m, n) for m, stream in enumerate(streams) for n in range(len(stream)))
        for _, m, n in order:
            streams[m][n]()

    halo_copy(FAR, 0).start()
    halo_copy(NEAR, 0).start()
    launch((2, 0), (3, 0))
    halo_copy(FAR, 1).start()
    halo_copy(NEAR, 1).start()
    launch((2, 1), (3, 1))
    launch((2, 2), (3, 2))
    launch((2, 3), (3, 3))
    fetch.start()
    for copy in factors:
        copy.wait()
    rows, cols = rows_ref[...], cols_ref[...]
    build_forward(sizes, rows, cols, fwd_high, fwd_low)
    build_bands(depth_ref[...].astype(jnp.float32), band, band_t)
    build_backward(sizes, rows, cols, bwd_high, bwd_low)
    home.wait()
    relay(FAR, 0)
    relay(NEAR, 0)
    halo_copy(FAR, 2).start()
    halo_copy(NEAR, 2).start()
    halo_copy(FAR, 3).start()
    halo_copy(NEAR, 3).start()
    middle(0, 2)
    relay(FAR, 1)
    relay(NEAR, 1)
    middle(2, 4)
    fetch.wait()
    arrived(FAR, 0, 2)
    arrived(NEAR, 0, 2)
    relay(FAR, 2)
    relay(NEAR, 2)
    mix(edges(0, 0, 2))
    mix(edges(1, 0, 2))
    mix(along_depth(0, 0))
    mix(along_depth(1, 0))
    mix(gradient(0, 0))
    mix(gradient(1, 0))
    mix(against_depth(0, 0))
    mix(against_depth(1, 0))
    relay(FAR, 3)
    relay(NEAR, 3)
    mix(corners(0, 0, 1))
    mix(corners(1, 0, 1))
    send_corners(FAR, 0, 1)
    send_corners(NEAR, 0, 1)
    arrived(FAR, 2, 3)
    arrived(NEAR, 2, 3)
    mix(edges(0, 2, 3))
    mix(edges(1, 2, 3))
    mix(along_depth(0, 1))
    mix(along_depth(1, 1))
    mix(gradient(0, 1))
    mix(gradient(1, 1))
    mix(against_depth(0, 1))
    mix(against_depth(1, 1))
    mix(corners(0, 1, 2))
    mix(corners(1, 1, 2))
    send_corners(FAR, 1, 2)
    send_corners(NEAR, 1, 2)
    strips(FAR, 0)
    strips(NEAR, 0)
    arrived(FAR, 3, 4)
    arrived(NEAR, 3, 4)
    mix(edges(0, 3, 4))
    mix(edges(1, 3, 4))
    mix(along_depth(0, 2))
    mix(along_depth(1, 2))
    mix(gradient(0, 2))
    mix(gradient(1, 2))
    mix(against_depth(0, 2))
    mix(against_depth(1, 2))
    mix(corners(0, 2, 4))
    mix(corners(1, 2, 4))
    send_corners(FAR, 2, 4)
    send_corners(NEAR, 2, 4)
    strips(FAR, 1)
    strips(NEAR, 1)
    sides(0, 2)
    strips(FAR, 2)
    strips(NEAR, 2)
    strips(FAR, 3)
    strips(NEAR, 3)
    sides(2, 4)
    final(0)
    final(1)
    final(2)
    final(3)
    for copy in list(copies.values()) + list(returns.values()):
        copy.wait_send()
    for c in range(chunks):
        for group in (0, 1):
            halo_copy(group, c).wait_send()
            strip_copy(group, c).wait_send()
            for copy in (*corner_copies(group, c), *return_copies(group, c)):
                copy.wait_send()


def per_device(tangent, hessian, kernel_rows, kernel_cols, kernel_depth):
    span_rows, span_cols, depth = tangent.shape
    reach = RADIUS
    ext_rows, ext_cols = span_rows + 2 * reach, span_cols + 2 * reach
    sizes = (span_rows, span_cols, ext_rows, ext_cols)
    counts = (lax.axis_size("gx"), lax.axis_size("gy"))
    own, wide = span_rows * span_cols, ext_rows * ext_cols
    groups, size, block = span_rows // reach, reach * span_cols, reach * ext_cols
    chunks = depth // LANES
    assert groups == 2 and chunks > 1 and counts[0] % 2 == 0
    full = pl.BlockSpec(memory_space=pltpu.VMEM)
    anywhere = pl.BlockSpec(memory_space=pl.ANY)
    bf16, f32 = jnp.bfloat16, jnp.float32
    return pl.pallas_call(
        lambda *refs: compute(sizes, counts, *refs),
        out_shape=pltpu.VMEM((span_rows, span_cols, depth), f32),
        in_specs=[anywhere] * 5,
        out_specs=full,
        scratch_shapes=[
            pltpu.VMEM((ext_rows, ext_cols, depth), f32),
            pltpu.VMEM((wide, depth), bf16),
            pltpu.VMEM((wide, depth), bf16),
            pltpu.VMEM((DENSITIES * size, 3 * block), bf16),
            pltpu.VMEM((DENSITIES * size, 3 * block), bf16),
            pltpu.VMEM((3 * block, DENSITIES * size), bf16),
            pltpu.VMEM((3 * block, DENSITIES * size), bf16),
            pltpu.VMEM((DENSITIES, WINDOW, WINDOW), bf16),
            pltpu.VMEM((DENSITIES, WINDOW, WINDOW), bf16),
            pltpu.VMEM((DENSITIES, DENSITIES, own, depth), bf16),
            pltpu.VMEM((groups, DENSITIES * size, depth), f32),
            pltpu.VMEM((groups, DENSITIES * size, depth), bf16),
            pltpu.VMEM((groups, DENSITIES * size, depth), f32),
            pltpu.VMEM((groups, DENSITIES * size, depth), bf16),
            pltpu.VMEM((groups, DENSITIES * size, LANES), f32),
            pltpu.VMEM((groups, DENSITIES * size, depth), bf16),
            pltpu.VMEM((groups, DENSITIES * size, depth), bf16),
            pltpu.VMEM((ext_rows, ext_cols, depth), f32),
            pltpu.VMEM((ext_rows, reach, depth), f32),
            pltpu.VMEM((ext_rows, reach, depth), f32),
            pltpu.VMEM((2, reach, span_cols, depth), f32),
            pltpu.VMEM(kernel_rows.shape, f32),
            pltpu.VMEM(kernel_cols.shape, f32),
            pltpu.VMEM(kernel_depth.shape, bf16),
            pltpu.SemaphoreType.DMA((5,)),
            pltpu.SemaphoreType.DMA((8, chunks)),
            pltpu.SemaphoreType.DMA((8, chunks)),
            pltpu.SemaphoreType.DMA((8, chunks)),
            pltpu.SemaphoreType.DMA((8, chunks)),
        ],
        compiler_params=pltpu.CompilerParams(
            vmem_limit_bytes=60 << 20, collective_id=0, has_side_effects=True),
    )(tangent, hessian.reshape(DENSITIES, DENSITIES, own, depth), kernel_rows, kernel_cols, kernel_depth)


def solution(mesh):
    return jax.shard_map(
        per_device,
        mesh=mesh,
        in_specs=(P("gx", "gy", None), P(None, None, "gx", "gy", None), P(), P(), P()),
        out_specs=P("gx", "gy", None),
        check_vma=False,
    )
```

```python
import jax
import jax.numpy as jnp
from jax import lax
from jax.experimental import pallas as pl
from jax.experimental.pallas import tpu as pltpu
from jax.sharding import PartitionSpec as P

RADIUS = 8
DENSITIES = 5
TAPS = 2 * RADIUS + 1
LANES = 128
WINDOW = 2 * LANES


def split(value):
    high = value.astype(jnp.bfloat16)
    low = (value - high.astype(jnp.float32)).astype(jnp.bfloat16)
    return high, low


def dot(left, right):
    return jnp.dot(left, right, preferred_element_type=jnp.float32)


def dot3(left_high, left_low, right_high, right_low):
    return dot(left_high, right_high) + dot(left_high, right_low) + dot(left_low, right_high)


def picked(taps, index):
    total = jnp.zeros(index.shape, jnp.float32)
    for tap in range(TAPS):
        weight = jnp.broadcast_to(taps[:, tap : tap + 1], index.shape)
        total = jnp.where(index == tap, weight, total)
    return total


def iota(shape, axis):
    return lax.broadcasted_iota(jnp.int32, shape, axis)


def build_forward(sizes, rows, cols, high_ref, low_ref):
    span_cols, ext_cols = sizes[1], sizes[3]
    wide = 3 * RADIUS * ext_cols
    row_index = iota((RADIUS, wide), 1) // ext_cols - iota((RADIUS, wide), 0)
    col_index = iota((span_cols, LANES), 1) % ext_cols - iota((span_cols, LANES), 0)
    for a in range(DENSITIES):
        by_row = picked(rows[a : a + 1], row_index)
        by_col = picked(cols[a : a + 1], col_index)
        by_col = jnp.concatenate([by_col] * (wide // LANES), axis=1)
        for r in range(RADIUS):
            at = pl.ds((a * RADIUS + r) * span_cols, span_cols)
            high_ref[at, :], low_ref[at, :] = split(by_row[r : r + 1, :] * by_col)


def build_backward(sizes, rows, cols, high_ref, low_ref):
    span_cols, ext_cols = sizes[1], sizes[3]
    size = RADIUS * span_cols
    row_index = iota((3 * RADIUS, size), 0) - iota((3 * RADIUS, size), 1) // span_cols
    col_index = iota((ext_cols, size), 0) - iota((ext_cols, size), 1) % span_cols
    for a in range(DENSITIES):
        by_row = picked(rows[a : a + 1], row_index)
        by_col = picked(cols[a : a + 1], col_index)
        into = pl.ds(a * size, size)
        for r in range(3 * RADIUS):
            at = pl.ds(r * ext_cols, ext_cols)
            high_ref[at, into], low_ref[at, into] = split(by_row[r : r + 1, :] * by_col)


def build_bands(depth_taps, band_ref, band_t_ref):
    step = 16
    shape = (step, WINDOW)
    offset = iota(shape, 0) - iota(shape, 1)
    for a in range(DENSITIES):
        taps = depth_taps[a : a + 1]
        for ref, sign in ((band_ref, 1), (band_t_ref, -1)):
            middle = picked(taps, sign * (offset + LANES) + RADIUS)
            for i in range(WINDOW // step):
                value = pltpu.roll(middle, (step * i - LANES) % WINDOW, 1)
                if i in (0, WINDOW // step - 1):
                    value = jnp.where(jnp.abs(offset + step * i) <= RADIUS, value, 0.0)
                ref[a, pl.ds(i * step, step), :] = value.astype(jnp.bfloat16)


def compute(sizes, counts, tangent_ref, hess_ref, rows_hbm, cols_hbm, depth_hbm, out_ref,
            ext, high, low, fwd_high, fwd_low, bwd_high, bwd_low, band, band_t, hess,
            acc, lateral, dens, lowered, pending, back_high, back_low, spread,
            from_left, from_right, from_ring, rows_ref, cols_ref, depth_ref,
            local_sems, send_sems, recv_sems, back_send_sems, back_recv_sems):
    span_rows, span_cols, ext_rows, ext_cols = sizes
    depth = acc.shape[-1]
    reach = RADIUS
    groups = span_rows // reach
    own, size, block = span_rows * span_cols, reach * span_cols, reach * ext_cols
    chunks = depth // LANES
    gx, gy = lax.axis_index("gx"), lax.axis_index("gy")
    left = {"gy": lax.rem(gy + counts[1] - 1, counts[1])}
    right = {"gy": lax.rem(gy + 1, counts[1])}
    mesh_ids = pl.DeviceIdType.MESH

    inner_rows, inner_cols = pl.ds(reach, span_rows), pl.ds(reach, span_cols)
    barrier = pltpu.get_barrier_semaphore()
    rings = [{"gx": lax.rem(gx + counts[0] + step, counts[0])} for step in (-1, 1)]
    for neighbour in (*rings, left, right):
        pl.semaphore_signal(barrier, inc=1, device_id=neighbour, device_id_type=mesh_ids)
    fetch = pltpu.make_async_copy(hess_ref, hess, local_sems.at[0])
    home = pltpu.make_async_copy(tangent_ref, ext.at[inner_rows, inner_cols, :], local_sems.at[1])
    home.start()
    factors = [pltpu.make_async_copy(source, target, local_sems.at[2 + n]) for n, (source, target) in enumerate(
        ((rows_hbm, rows_ref), (cols_hbm, cols_ref), (depth_hbm, depth_ref)))]
    for copy in factors:
        copy.start()
    pl.semaphore_wait(barrier, 4)

    first_cols, last_cols = pl.ds(0, reach), pl.ds(reach + span_cols, reach)
    near_first, near_last = pl.ds(reach, reach), pl.ds(span_cols, reach)
    lanes = [pl.ds(c * LANES, LANES) for c in range(chunks)]

    def remote(source, target, send_sem, recv_sem, device):
        return pltpu.make_async_remote_copy(
            src_ref=source, dst_ref=target, send_sem=send_sem, recv_sem=recv_sem,
            device_id=device, device_id_type=mesh_ids)

    head_cols, tail_cols = pl.ds(0, reach), pl.ds(span_cols - reach, reach)
    every_row, every_col = pl.ds(0, span_rows), pl.ds(0, span_cols)
    copies, returns = {}, {}
    for c, z in enumerate(lanes):
        plan = [
            (tangent_ref.at[every_row, tail_cols, z], ext.at[inner_rows, first_cols, z], right),
            (tangent_ref.at[every_row, head_cols, z], ext.at[inner_rows, last_cols, z], left),
        ]
        for side, (source, target, device) in enumerate(plan):
            copies[2 + side, c] = remote(source, target, send_sems.at[2 + side, c], recv_sems.at[2 + side, c], device)
        plan = [
            (spread.at[inner_rows, last_cols, z], from_left.at[inner_rows, :, z], right),
            (spread.at[inner_rows, first_cols, z], from_right.at[inner_rows, :, z], left),
        ]
        for side, (source, target, device) in enumerate(plan):
            returns[4 + side, c] = remote(source, target, back_send_sems.at[4 + side, c], back_recv_sems.at[4 + side, c], device)

    odd = lax.rem(gx, 2)
    FAR, NEAR = odd, 1 - odd

    def ring(group):
        return {"gx": lax.rem(gx + counts[0] - 1 + 2 * group, counts[0])}

    def halo(group):
        return pl.ds(group * (reach + span_rows), reach)

    def halo_copy(group, c):
        z = lanes[c]
        source = tangent_ref.at[pl.ds(group * (span_rows - reach), reach), every_col, z]
        return remote(source, ext.at[halo(1 - group), inner_cols, z], send_sems.at[1 - group, c], recv_sems.at[1 - group, c], ring(group))

    def corner_copies(group, c):
        z, rows_at = lanes[c], halo(group)
        for side, near, far, device in ((0, near_last, first_cols, right), (1, near_first, last_cols, left)):
            kind = 4 + 2 * group + side
            yield remote(ext.at[rows_at, near, z], ext.at[rows_at, far, z], send_sems.at[kind, c], recv_sems.at[kind, c], device)

    def return_copies(group, c):
        z, rows_at = lanes[c], halo(group)
        for side, cols_at, target, device in ((0, last_cols, from_left, right), (1, first_cols, from_right, left)):
            kind = 2 * group + side
            yield remote(spread.at[rows_at, cols_at, z], target.at[rows_at, :, z], back_send_sems.at[kind, c], back_recv_sems.at[kind, c], device)

    def strip_copy(group, c):
        z, kind = lanes[c], 6 + group
        return remote(spread.at[halo(group), inner_cols, z], from_ring.at[1 - group, :, :, z], back_send_sems.at[kind, c], back_recv_sems.at[kind, c], ring(group))

    def launch(*pairs):
        for kind, c in pairs:
            copies[kind, c].start()

    def relay(group, c):
        halo_copy(1 - group, c).wait_recv()
        for copy in corner_copies(group, c):
            copy.start()

    def at_lanes(begin, end):
        return pl.ds(begin * LANES, (end - begin) * LANES)

    def prepare(z, start, count):
        value = ext[pl.ds(start, count), :, z].reshape(count * ext_cols, z.size)
        at = pl.ds(start * ext_cols, count * ext_cols)
        high[at, z], low[at, z] = split(value)

    def middle(begin, end):
        z = at_lanes(begin, end)
        for c in range(begin, end):
            copies[2, c].wait_recv()
            copies[3, c].wait_recv()
        prepare(z, reach, span_rows)
        data = pl.ds(block, 2 * block)
        for group in (0, 1):
            weights = pl.ds((1 - group) * block, 2 * block)
            acc[group, :, z] = dot3(fwd_high[:, weights], fwd_low[:, weights], high[data, z], low[data, z])

    def arrived(group, begin, end):
        for c in range(begin, end):
            for copy in corner_copies(group, c):
                copy.wait_recv()

    def edges(group, begin, end):
        def emit():
            z = at_lanes(begin, end)
            prepare(z, group * (reach + span_rows), reach)
            weights, data = pl.ds(group * 2 * block, block), pl.ds(group * 3 * block, block)
            total = acc[group, :, z] + dot3(fwd_high[:, weights], fwd_low[:, weights], high[data, z], low[data, z])
            lateral[group, :, z] = total.astype(jnp.bfloat16)

        return [emit]

    keep = iota((size, LANES), 1) < LANES // 2

    def along_depth(group, k):
        z, here, ahead = pl.ds(k * LANES, WINDOW), lanes[k], lanes[k + 1]

        def emit(a):
            part = pl.ds(a * size, size)
            value = dot(lateral[group, part, z], band[a])
            begin = value[:, :LANES]
            dens[group, part, here] = begin if k == 0 else jnp.where(keep, dens[group, part, here], begin)
            dens[group, part, ahead] = value[:, LANES:]

        return [lambda a=a: emit(a) for a in range(DENSITIES)]

    def gradient(group, k):
        step = 16

        def emit(r, z):
            at = pl.ds(group * size + r * step, step)
            values = [dens[group, pl.ds(b * size + r * step, step), z] for b in range(DENSITIES)]
            for a in range(DENSITIES):
                total = None
                for b in range(DENSITIES):
                    term = hess[a, b, at, z].astype(jnp.float32) * values[b]
                    total = term if total is None else total + term
                lowered[group, pl.ds(a * size + r * step, step), z] = total.astype(jnp.bfloat16)

        return [lambda r=r, z=z: emit(r, z) for r in range(size // step) for z in (lanes[k], lanes[k + 1])]

    def against_depth(group, k):
        z, here, ahead = pl.ds(k * LANES, WINDOW), lanes[k], lanes[k + 1]

        def emit(a):
            part = pl.ds(a * size, size)
            value = dot(lowered[group, part, z], band_t[a])
            begin, rest = value[:, :LANES], value[:, LANES:]
            if k > 0:
                begin = jnp.where(keep, pending[group, part, :], begin)
            back_high[group, part, here], back_low[group, part, here] = split(begin)
            if k == chunks - 2:
                back_high[group, part, ahead], back_low[group, part, ahead] = split(rest)
            else:
                pending[group, part, :] = rest

        return [lambda a=a: emit(a) for a in range(DENSITIES)]

    def corners(group, begin, end):
        def emit():
            z = at_lanes(begin, end)
            part = pl.ds(group * 2 * block, block)
            value = dot3(bwd_high[part, :], bwd_low[part, :], back_high[group, :, z], back_low[group, :, z])
            spread[halo(group), :, z] = value.reshape(reach, ext_cols, z.size)

        return [emit]

    def send_corners(group, begin, end):
        for c in range(begin, end):
            for copy in return_copies(group, c):
                copy.start()

    def sides(begin, end):
        z = at_lanes(begin, end)
        for index in (0, 1):
            total = None
            for group in (0, 1):
                part = pl.ds((1 + index - group) * block, block)
                term = dot3(bwd_high[part, :], bwd_low[part, :], back_high[group, :, z], back_low[group, :, z])
                total = term if total is None else total + term
            spread[pl.ds((1 + index) * reach, reach), :, z] = total.reshape(reach, ext_cols, z.size)
        for c in range(begin, end):
            for kind in (4, 5):
                returns[kind, c].start()

    def strips(group, c):
        z, rows_at = lanes[c], halo(group)
        for copy in return_copies(group, c):
            copy.wait_recv()
        spread[rows_at, near_first, z] = spread[rows_at, near_first, z] + from_left[rows_at, :, z]
        spread[rows_at, near_last, z] = spread[rows_at, near_last, z] + from_right[rows_at, :, z]
        strip_copy(group, c).start()

    def final(c):
        z = lanes[c]
        for kind in (4, 5):
            returns[kind, c].wait_recv()
        spread[inner_rows, near_first, z] = spread[inner_rows, near_first, z] + from_left[inner_rows, :, z]
        spread[inner_rows, near_last, z] = spread[inner_rows, near_last, z] + from_right[inner_rows, :, z]
        for group in (0, 1):
            strip_copy(1 - group, c).wait_recv()
            edge, rows_at = pl.ds(reach + group * reach, reach), pl.ds(group * reach, reach)
            out_ref[rows_at, :, z] = spread[edge, inner_cols, z] + from_ring[group, :, :, z]

    def mix(*streams):
        order = sorted(((n + 0.5) / len(stream), m, n) for m, stream in enumerate(streams) for n in range(len(stream)))
        for _, m, n in order:
            streams[m][n]()

    halo_copy(FAR, 0).start()
    halo_copy(NEAR, 0).start()
    launch((2, 0), (3, 0))
    halo_copy(FAR, 1).start()
    halo_copy(NEAR, 1).start()
    launch((2, 1), (3, 1))
    launch((2, 2), (3, 2))
    launch((2, 3), (3, 3))
    fetch.start()
    for copy in factors:
        copy.wait()
    rows, cols = rows_ref[...], cols_ref[...]
    build_forward(sizes, rows, cols, fwd_high, fwd_low)
    build_bands(depth_ref[...].astype(jnp.float32), band, band_t)
    build_backward(sizes, rows, cols, bwd_high, bwd_low)
    home.wait()
    relay(FAR, 0)
    relay(NEAR, 0)
    halo_copy(FAR, 2).start()
    halo_copy(NEAR, 2).start()
    halo_copy(FAR, 3).start()
    halo_copy(NEAR, 3).start()
    middle(0, 2)
    relay(FAR, 1)
    relay(NEAR, 1)
    middle(2, 4)
    fetch.wait()
    arrived(FAR, 0, 2)
    arrived(NEAR, 0, 2)
    relay(FAR, 2)
    relay(NEAR, 2)
    mix(edges(0, 0, 2))
    mix(edges(1, 0, 2))
    mix(along_depth(0, 0))
    mix(along_depth(1, 0))
    mix(gradient(0, 0))
    mix(gradient(1, 0))
    relay(FAR, 3)
    relay(NEAR, 3)
    mix(against_depth(0, 0))
    mix(against_depth(1, 0))
    mix(corners(0, 0, 1))
    mix(corners(1, 0, 1))
    send_corners(FAR, 0, 1)
    send_corners(NEAR, 0, 1)
    arrived(FAR, 2, 3)
    arrived(NEAR, 2, 3)
    mix(edges(0, 2, 3))
    mix(edges(1, 2, 3))
    mix(along_depth(0, 1))
    mix(along_depth(1, 1))
    mix(gradient(0, 1))
    mix(gradient(1, 1))
    mix(against_depth(0, 1))
    mix(against_depth(1, 1))
    mix(corners(0, 1, 2))
    mix(corners(1, 1, 2))
    send_corners(FAR, 1, 2)
    send_corners(NEAR, 1, 2)
    strips(FAR, 0)
    strips(NEAR, 0)
    arrived(FAR, 3, 4)
    arrived(NEAR, 3, 4)
    mix(edges(0, 3, 4))
    mix(edges(1, 3, 4))
    mix(along_depth(0, 2))
    mix(along_depth(1, 2))
    mix(gradient(0, 2))
    mix(gradient(1, 2))
    mix(against_depth(0, 2))
    mix(against_depth(1, 2))
    mix(corners(0, 2, 4))
    mix(corners(1, 2, 4))
    send_corners(FAR, 2, 4)
    send_corners(NEAR, 2, 4)
    strips(FAR, 1)
    strips(NEAR, 1)
    sides(0, 2)
    strips(FAR, 2)
    strips(NEAR, 2)
    strips(FAR, 3)
    strips(NEAR, 3)
    sides(2, 4)
    final(0)
    final(1)
    final(2)
    final(3)
    for copy in list(copies.values()) + list(returns.values()):
        copy.wait_send()
    for c in range(chunks):
        for group in (0, 1):
            halo_copy(group, c).wait_send()
            strip_copy(group, c).wait_send()
            for copy in (*corner_copies(group, c), *return_copies(group, c)):
                copy.wait_send()


def per_device(tangent, hessian, kernel_rows, kernel_cols, kernel_depth):
    span_rows, span_cols, depth = tangent.shape
    reach = RADIUS
    ext_rows, ext_cols = span_rows + 2 * reach, span_cols + 2 * reach
    sizes = (span_rows, span_cols, ext_rows, ext_cols)
    counts = (lax.axis_size("gx"), lax.axis_size("gy"))
    own, wide = span_rows * span_cols, ext_rows * ext_cols
    groups, size, block = span_rows // reach, reach * span_cols, reach * ext_cols
    chunks = depth // LANES
    assert groups == 2 and chunks > 1 and counts[0] % 2 == 0
    full = pl.BlockSpec(memory_space=pltpu.VMEM)
    anywhere = pl.BlockSpec(memory_space=pl.ANY)
    bf16, f32 = jnp.bfloat16, jnp.float32
    return pl.pallas_call(
        lambda *refs: compute(sizes, counts, *refs),
        out_shape=pltpu.VMEM((span_rows, span_cols, depth), f32),
        in_specs=[anywhere] * 5,
        out_specs=full,
        scratch_shapes=[
            pltpu.VMEM((ext_rows, ext_cols, depth), f32),
            pltpu.VMEM((wide, depth), bf16),
            pltpu.VMEM((wide, depth), bf16),
            pltpu.VMEM((DENSITIES * size, 3 * block), bf16),
            pltpu.VMEM((DENSITIES * size, 3 * block), bf16),
            pltpu.VMEM((3 * block, DENSITIES * size), bf16),
            pltpu.VMEM((3 * block, DENSITIES * size), bf16),
            pltpu.VMEM((DENSITIES, WINDOW, WINDOW), bf16),
            pltpu.VMEM((DENSITIES, WINDOW, WINDOW), bf16),
            pltpu.VMEM((DENSITIES, DENSITIES, own, depth), bf16),
            pltpu.VMEM((groups, DENSITIES * size, depth), f32),
            pltpu.VMEM((groups, DENSITIES * size, depth), bf16),
            pltpu.VMEM((groups, DENSITIES * size, depth), f32),
            pltpu.VMEM((groups, DENSITIES * size, depth), bf16),
            pltpu.VMEM((groups, DENSITIES * size, LANES), f32),
            pltpu.VMEM((groups, DENSITIES * size, depth), bf16),
            pltpu.VMEM((groups, DENSITIES * size, depth), bf16),
            pltpu.VMEM((ext_rows, ext_cols, depth), f32),
            pltpu.VMEM((ext_rows, reach, depth), f32),
            pltpu.VMEM((ext_rows, reach, depth), f32),
            pltpu.VMEM((2, reach, span_cols, depth), f32),
            pltpu.VMEM(kernel_rows.shape, f32),
            pltpu.VMEM(kernel_cols.shape, f32),
            pltpu.VMEM(kernel_depth.shape, bf16),
            pltpu.SemaphoreType.DMA((5,)),
            pltpu.SemaphoreType.DMA((8, chunks)),
            pltpu.SemaphoreType.DMA((8, chunks)),
            pltpu.SemaphoreType.DMA((8, chunks)),
            pltpu.SemaphoreType.DMA((8, chunks)),
        ],
        compiler_params=pltpu.CompilerParams(
            vmem_limit_bytes=60 << 20, collective_id=0, has_side_effects=True),
    )(tangent, hessian.reshape(DENSITIES, DENSITIES, own, depth), kernel_rows, kernel_cols, kernel_depth)


def solution(mesh):
    return jax.shard_map(
        per_device,
        mesh=mesh,
        in_specs=(P("gx", "gy", None), P(None, None, "gx", "gy", None), P(), P(), P()),
        out_specs=P("gx", "gy", None),
        check_vma=False,
    )
```
